512 devices in a mesh: tm: 32 (over z, x), tile: 16 (over y, core).
Axes of the slice: x: 4, y: 8, z: 8, core: 2. Of those that a mesh axis runs over, the one named last changes fastest.
Arguments:
- features: bfloat16 [32, 32, 160, 512], P('tm', 'tile'), may hold values from -200 to 200, as said below
- norm_gain: float32 [512], replicated, may hold values from 0.1 to 1.9
- query_weight: bfloat16 [512, 512], replicated, may hold values from -7.9991455 to 7.9991455, as said below
- key_weight: bfloat16 [512, 512], replicated, may hold values from -0.25 to 0.25
- value_weight: bfloat16 [512, 512], replicated, may hold values from -0.25 to 0.25
- out_weight: bfloat16 [512, 512], replicated, may hold values from -0.5 to 0.5
- conv_weight: bfloat16 [3, 3, 3, 512, 256], replicated, may hold values from -0.0546875 to 0.0546875
- skip_weight: bfloat16 [512, 256], replicated, may hold values from -0.125 to 0.125
Outputs:
- decoded: bfloat16 [64, 32, 160, 256], P('tm', 'tile')
The draws below stay inside these ranges and needn't reach their ends.
Inputs may be any that keep to these rules, and one draw needn't show every extreme that they name: Latent features whose magnitude varies from row to row and column to column. `query_weight`: A dense projection matrix.
All inputs are finite; a program needn't handle non-finite values.
Results may differ from the reference program's by a relative error of at most 0.012.
The reference program's roundings to bfloat16 on the way (of `normed`, `weights`, `attended`, `mid` and `act`) count: a program that leaves them out, or rounds other values in their place, can miss the bound.
Values may be sent and summed in bfloat16 or wider, within the bound.
A program may use at most 128 MiB of HBM per device.

```python
import jax
import jax.numpy as jnp
from jax import lax

C = 512
C2 = 256
GROUPS = 32
COLS = 160
FRAMES = 32
ROWS = 32


def draw_features(key, part):
    first_key, second_key, third_key = jax.random.split(key, 3)
    shape = (FRAMES, ROWS, COLS, C)
    row_scale = (3.0 ** (jnp.arange(ROWS, dtype=jnp.float32) / max(ROWS - 1, 1))).reshape(1, ROWS, 1, 1)
    col_scale = jnp.exp(jax.random.uniform(second_key, (1, 1, COLS, 1)) * jnp.log(3.5))
    chan_scale = jnp.exp(jax.random.uniform(third_key, (1, 1, 1, C)) * jnp.log(2.0))
    base = jnp.clip(jax.random.normal(first_key, shape), -5.0, 5.0)
    return jnp.clip(base * row_scale * col_scale * chan_scale, -200.0, 200.0).astype(jnp.bfloat16)


def draw_query_weight(key, part):
    values = jnp.clip(jax.random.normal(key, (C, C)), -6.0, 6.0) * C ** (-0.5)
    return values.astype(jnp.bfloat16)


def normal_values(rng, extent, spread, most, kind=jnp.bfloat16):
    array = spread * jax.random.normal(rng, extent, jnp.float32)
    return jnp.clip(array, min=-most, max=most).astype(kind)


def setup_inputs(seed: int = 0) -> dict:
    streams_of = jax.random.split(jax.random.key(seed), 9)
    features = draw_features(jax.random.fold_in(streams_of[8], 71), 0)
    norm_gain = jnp.clip(1.0 + 0.18 * jax.random.normal(streams_of[1], (C,), jnp.float32), 0.1, 1.9)
    query_weight = draw_query_weight(jax.random.fold_in(streams_of[8], 71), 0)
    key_weight = normal_values(streams_of[3], (C, C), C ** -0.5, 0.25)
    value_weight = normal_values(streams_of[4], (C, C), C ** -0.5, 0.25)
    out_weight = normal_values(streams_of[5], (C, C), (C // 4) ** -0.5, 0.5)
    conv_weight = normal_values(streams_of[6], (3, 3, 3, C, C2), (27 * C) ** -0.5, 0.0546875)
    skip_weight = normal_values(streams_of[7], (C, C2), (4 * C) ** -0.5, 0.125)
    return {"features": features, "norm_gain": norm_gain, "query_weight": query_weight, "key_weight": key_weight, "value_weight": value_weight, "out_weight": out_weight, "conv_weight": conv_weight, "skip_weight": skip_weight}


def frame_patches(frame):
    padded = jnp.pad(frame, ((1, 1), (1, 1), (0, 0)))
    pieces = [padded[offset_y:offset_y + ROWS, offset_x:offset_x + COLS, :] for offset_y in range(3) for offset_x in range(3)]
    return jnp.concatenate(pieces, axis=-1).reshape(ROWS * COLS, 9 * C)

def reference(features, norm_gain, query_weight, key_weight, value_weight, out_weight, conv_weight, skip_weight):
    cell_count = ROWS * COLS
    grouped = features.astype(jnp.float32).reshape(FRAMES, cell_count, GROUPS, C // GROUPS)
    mean = lax.optimization_barrier(jnp.mean(grouped, axis=(1, 3), keepdims=True))
    var = lax.optimization_barrier(jnp.mean(grouped * grouped, axis=(1, 3), keepdims=True)) - mean * mean
    normed = ((grouped - mean) * lax.rsqrt(var + 1e-06)).reshape(FRAMES, cell_count, C) * norm_gain
    normed = normed.astype(jnp.bfloat16)

    def attend(frame_normed):
        queries = jnp.dot(frame_normed, query_weight, preferred_element_type=jnp.float32).astype(jnp.bfloat16)
        key_rows = jnp.dot(frame_normed, key_weight, preferred_element_type=jnp.float32).astype(jnp.bfloat16)
        value_rows = jnp.dot(frame_normed, value_weight, preferred_element_type=jnp.float32).astype(jnp.bfloat16)
        scores = jnp.dot(queries, key_rows.T, preferred_element_type=jnp.float32) * C ** (-0.5)
        peak = lax.optimization_barrier(jnp.max(scores, axis=1, keepdims=True))
        unnormed = jnp.exp(scores - peak)
        denominator = lax.optimization_barrier(jnp.sum(unnormed, axis=1, keepdims=True))
        weights = unnormed.astype(jnp.bfloat16)
        attended = (jnp.dot(weights, value_rows, preferred_element_type=jnp.float32) / denominator).astype(jnp.bfloat16)
        return jnp.dot(attended, out_weight, preferred_element_type=jnp.float32)
    change = lax.map(attend, normed)
    mid = (features.astype(jnp.float32).reshape(FRAMES, cell_count, C) + change).astype(jnp.bfloat16)
    act = jax.nn.silu(mid.astype(jnp.float32)).astype(jnp.bfloat16).reshape(FRAMES, ROWS, COLS, C)
    before_all = jnp.concatenate([act[:1], act[:-1]], axis=0)
    taps = conv_weight.reshape(3, 9 * C, C2)

    def decode(packed):
        before, current, mid_frame = packed
        patch_before = frame_patches(before)
        patch_now = frame_patches(current)
        skip = jnp.dot(mid_frame, skip_weight, preferred_element_type=jnp.float32)
        first_tap = jnp.dot(patch_before, taps[0], preferred_element_type=jnp.float32)
        even = first_tap + jnp.dot(patch_before, taps[1], preferred_element_type=jnp.float32) + jnp.dot(patch_now, taps[2], preferred_element_type=jnp.float32) + skip
        odd = first_tap + jnp.dot(patch_now, taps[1], preferred_element_type=jnp.float32) + jnp.dot(patch_now, taps[2], preferred_element_type=jnp.float32) + skip
        return jnp.stack([even, odd], axis=0).astype(jnp.bfloat16)
    decoded = lax.map(decode, (before_all, act, mid))
    return decoded.reshape(2 * FRAMES, ROWS, COLS, C2)
```

```python
import functools
import math

import jax
import jax.numpy as jnp
from jax import lax
from jax.experimental import pallas as pl
from jax.experimental.pallas import tpu as pltpu
from jax.sharding import PartitionSpec as P

GROUPS = 32
EPS = 1e-06
MESH = pl.DeviceIdType.MESH
F32 = jnp.float32
BF16 = jnp.bfloat16


def group_sum(v, width):
    lanes = v.shape[-1]
    lane = lax.broadcasted_iota(jnp.int32, v.shape, 1)
    step = 1
    while step < width:
        above = pltpu.roll(v, lanes - step, 1)
        below = pltpu.roll(v, step, 1)
        v = v + jnp.where((lane & step) == 0, above, below)
        step *= 2
    return v


def kernel(
    spans, tiles, x_hbm, gain_ref, wq_hbm, wk_hbm, wv_hbm, wo_hbm, wc_hbm, ws_hbm,
    out_ref,
    slots, q2, acc, peak, total, stats, mid, act, even, odd, ab,
    wq, wk, wv, wo, wc, ws,
    ring_send, ring_recv, sib_send, sib_recv, st_send, st_recv, edge_send, edge_recv, load_sem, conv_sem,
):
    rows, cols, channels = x_hbm.shape
    cells = rows * cols
    out_channels = ws.shape[1]
    width = channels // GROUPS
    blocks = channels // 128
    chips = tiles // 2
    steps = chips

    t = lax.axis_index("tm")
    i = lax.axis_index("tile")
    y = i // 2
    core = i - 2 * y
    right = lax.rem(i + 2, tiles)
    left = lax.rem(i + tiles - 2, tiles)
    sibling = 2 * y + 1 - core
    above = lax.rem(i + tiles - 1, tiles)
    below = lax.rem(i + 1, tiles)
    t_next = lax.rem(t + 1, spans)
    t_prev = lax.rem(t + spans - 1, spans)

    def remote(src, dst, send, recv, where):
        return pltpu.make_async_remote_copy(
            src_ref=src, dst_ref=dst, send_sem=send, recv_sem=recv, device_id=where, device_id_type=MESH
        )

    loads = [
        pltpu.make_async_copy(x_hbm, slots.at[0, pl.ds(0, 2)], load_sem.at[0]),
        pltpu.make_async_copy(wq_hbm, wq, load_sem.at[1]),
        pltpu.make_async_copy(wk_hbm, wk, load_sem.at[2]),
        pltpu.make_async_copy(wv_hbm, wv, load_sem.at[3]),
        pltpu.make_async_copy(wo_hbm, wo, load_sem.at[4]),
        pltpu.make_async_copy(ws_hbm, ws, load_sem.at[5]),
    ]
    loads[0].start()

    barrier = pltpu.get_barrier_semaphore()

    def greet(k, carry):
        pl.semaphore_signal(barrier, inc=1, device_id=(t, lax.rem(i + k, tiles)), device_id_type=MESH)
        return carry

    lax.fori_loop(1, tiles, greet, 0)
    pl.semaphore_signal(barrier, inc=1, device_id=(t_next, i), device_id_type=MESH)
    pl.semaphore_signal(barrier, inc=1, device_id=(t_prev, i), device_id_type=MESH)
    pl.semaphore_wait(barrier, tiles + 1)

    def first(h, lane):
        row = h if lane == 0 else 1 - h
        return remote(
            x_hbm.at[row], slots.at[1 + h, lane], ring_send.at[1 + h, lane], ring_recv.at[1 + h, lane],
            (t, right if lane == 0 else left),
        )

    for h in range(2):
        for lane in range(2):
            first(h, lane).start()
    own_to_sibling = remote(
        x_hbm, slots.at[0, pl.ds(2, 2)], sib_send.at[0], sib_recv.at[0], (t, sibling)
    )
    own_to_sibling.start()

    for copy in loads[1:]:
        copy.start()

    def load_tap(k, carry):
        dt = k // 9
        dy = (k - 9 * dt) // 3
        dx = k - 9 * dt - 3 * dy
        column = pl.multiple_of(dt * out_channels, out_channels)
        pltpu.make_async_copy(
            wc_hbm.at[dt, dy, dx], wc.at[dx, dy, :, pl.ds(column, out_channels)], conv_sem.at[k]
        ).start()
        return carry

    lax.fori_loop(0, 27, load_tap, 0)

    loads[0].wait()
    own = slots[0, 0:2].reshape(cells, channels).astype(F32)
    sums = jnp.sum(own, axis=0, keepdims=True)
    squares = jnp.sum(own * own, axis=0, keepdims=True)
    sums = group_sum(jnp.broadcast_to(sums, (8, channels)), width)
    squares = group_sum(jnp.broadcast_to(squares, (8, channels)), width)
    lane_of = lax.broadcasted_iota(jnp.int32, (8, 128), 1) & (width - 1)
    packed = jnp.zeros((8, 128), F32)
    for k in range(2 * blocks):
        source = sums if k < blocks else squares
        b = k % blocks
        packed = jnp.where(lane_of == k, source[:, b * 128:(b + 1) * 128], packed)
    stats[0] = packed[0:1]

    def stat_copy(k):
        return remote(
            stats.at[0], stats.at[k], st_send.at[k], st_recv.at[k], (t, lax.rem(i + k, tiles))
        )

    def send_stat(k, carry):
        stat_copy(k).start()
        return carry

    lax.fori_loop(1, tiles, send_stat, 0)

    def ring_copy(e, lane):
        return remote(
            slots.at[e, lane], slots.at[e + 2, lane], ring_send.at[e + 2, lane], ring_recv.at[e + 2, lane],
            (t, right if lane == 0 else left),
        )

    def ring_arrival(e, lane):
        return remote(
            slots.at[e, lane], slots.at[e, lane], ring_send.at[e, lane], ring_recv.at[e, lane],
            (t, right if lane == 0 else left),
        )

    def sib_copy(e):
        return remote(
            slots.at[e, pl.ds(0, 2)], slots.at[e, pl.ds(2, 2)], sib_send.at[e], sib_recv.at[e], (t, sibling)
        )

    def prepare():
        def take(k, carry):
            stat_copy(k).wait_recv()
            return carry

        lax.fori_loop(1, tiles, take, 0)
        whole = stats[0]
        for k in range(1, tiles):
            whole = whole + stats[k]
        whole = jnp.broadcast_to(whole, (8, 128))
        spread = [group_sum(jnp.where(lane_of == k, whole, 0.0), width) for k in range(2 * blocks)]
        population = float(tiles * cells * width)
        mean = jnp.concatenate(spread[:blocks], axis=1)[0:1] / population
        var = jnp.concatenate(spread[blocks:], axis=1)[0:1] / population - mean * mean
        rstd = lax.rsqrt(var + EPS)
        gain = gain_ref[...]
        ab[0:1] = rstd * gain
        ab[1:2] = -mean * rstd * gain
        block = slots[0, 0:2].reshape(cells, channels).astype(F32)
        normed = (((block - mean) * rstd) * gain).astype(BF16)
        loads[1].wait()
        queries = jnp.dot(normed, wq[...], preferred_element_type=F32).astype(BF16)
        loads[2].wait()
        inner = lax.dot_general(queries, wk[...], (((1,), (1,)), ((), ())), preferred_element_type=F32)
        scale = channels ** (-0.5) * math.log2(math.e)
        q2[...] = (inner * (rstd * gain * scale)).astype(BF16)
        acc[...] = jnp.zeros_like(acc)
        total[...] = jnp.zeros_like(total)
        peak[...] = jnp.full_like(peak, -jnp.inf)

    def attend(e):
        keys = slots[e].reshape(4 * cols, channels)
        scores = lax.dot_general(q2[...], keys, (((1,), (1,)), ((), ())), preferred_element_type=F32)
        before = peak[:, 0:1]
        now = jnp.maximum(before, jnp.max(scores, axis=1, keepdims=True))
        fade = jnp.exp2(before - now)
        weights = jnp.exp2(scores - now).astype(BF16)
        peak[...] = jnp.broadcast_to(now, peak.shape)
        total[...] = total[...] * fade + jnp.sum(weights.astype(F32), axis=1, keepdims=True)
        acc[...] = acc[...] * fade + jnp.dot(weights, keys, preferred_element_type=F32)

    def gather_step(e, carry):
        @pl.when(e < steps - 1)
        def _():
            for lane in range(2):
                ring_arrival(e + 1, lane).wait_recv()

                @pl.when(e < steps - 3)
                def _():
                    ring_copy(e + 1, lane).start()

            sib_copy(e + 1).start()

        @pl.when(e == 0)
        def _():
            prepare()

        sib_copy(e).wait_recv()
        attend(e)
        return carry

    lax.fori_loop(0, steps, gather_step, 0)

    loads[3].wait()
    loads[4].wait()

    def halo_up(which):
        return remote(
            act.at[which, 1], act.at[which, 3], edge_send.at[2 * which], edge_recv.at[2 * which], (t, above)
        )

    def halo_down(which):
        return remote(
            act.at[which, 2], act.at[which, 0], edge_send.at[2 * which + 1], edge_recv.at[2 * which + 1], (t, below)
        )

    def onward(row):
        return remote(
            act.at[0, 1 + row], act.at[1, 1 + row], edge_send.at[4 + row], edge_recv.at[4 + row], (t_next, i)
        )

    def finish(k, carry):
        row = k + core - 2 * k * core
        part = pl.ds(pl.multiple_of(row * cols, cols), cols)
        mixed = acc[part, :] * (1.0 / total[part, 0:1])
        mixed = (mixed * ab[0:1] + ab[1:2]).astype(BF16)
        attended = jnp.dot(mixed, wv[...], preferred_element_type=F32).astype(BF16)
        change = jnp.dot(attended, wo[...], preferred_element_type=F32)
        mid_row = (slots[0, row].astype(F32) + change).astype(BF16)
        mid[part, :] = mid_row
        wide = mid_row.astype(F32)
        act[0, 1 + row] = (wide * (1.0 / (1.0 + jnp.exp(-wide)))).astype(BF16)
        onward(row).start()

        @pl.when(row == 0)
        def _():
            halo_up(0).start()

        @pl.when(row == 1)
        def _():
            halo_down(0).start()

        return carry

    lax.fori_loop(0, 2, finish, 0)

    loads[5].wait()

    def tap_wait(k, carry):
        dt = k // 9
        dy = (k - 9 * dt) // 3
        dx = k - 9 * dt - 3 * dy
        column = pl.multiple_of(dt * out_channels, out_channels)
        pltpu.make_async_copy(
            wc_hbm.at[dt, dy, dx], wc.at[dx, dy, :, pl.ds(column, out_channels)], conv_sem.at[k]
        ).wait()
        return carry

    lax.fori_loop(0, 27, tap_wait, 0)
    skip = jnp.dot(mid[...], ws[...], preferred_element_type=F32)
    even[...] = skip
    odd[...] = skip
    position = lax.rem(lax.broadcasted_iota(jnp.int32, (cells, 1), 0), cols)

    def product(which, dx, start):
        z = None
        for dy in range(3):
            piece = act[which, dy:dy + 2].reshape(cells, channels)
            part = jnp.dot(piece, wc[dx, dy, :, start:start + 2 * out_channels], preferred_element_type=F32)
            z = part if z is None else z + part
        if dx == 0:
            z = jnp.where(position == 0, 0.0, pltpu.roll(z, 1, 0))
        if dx == 2:
            z = jnp.where(position == cols - 1, 0.0, pltpu.roll(z, cells - 1, 0))
        return z[:, :out_channels], z[:, out_channels:]

    def clear(which):
        @pl.when(i == 0)
        def _():
            act[which, 0] = jnp.zeros((cols, channels), BF16)

        @pl.when(i == tiles - 1)
        def _():
            act[which, 3] = jnp.zeros((cols, channels), BF16)

    halo_up(0).wait_recv()
    halo_down(0).wait_recv()
    clear(0)
    for dx in range(3):
        second, third = product(0, dx, out_channels)
        even[...] += third
        odd[...] += second + third

    def pass_on(k, carry):
        row = k + core - 2 * k * core
        onward(row).wait_recv()

        @pl.when(row == 0)
        def _():
            halo_up(1).start()

        @pl.when(row == 1)
        def _():
            halo_down(1).start()

        return carry

    lax.fori_loop(0, 2, pass_on, 0)
    halo_up(1).wait_recv()
    halo_down(1).wait_recv()
    clear(1)
    which = jnp.where(t == 0, 0, 1)
    for dx in range(3):
        one, second = product(which, dx, 0)
        even[...] += one + second
        odd[...] += one
    out_ref[0] = even[...].astype(BF16)
    out_ref[1] = odd[...].astype(BF16)

    for h in range(2):
        for lane in range(2):
            first(h, lane).wait_send()
    own_to_sibling.wait_send()

    def drain(e, carry):
        for lane in range(2):
            @pl.when(e < steps - 2)
            def _():
                ring_copy(e, lane).wait_send()
        sib_copy(e).wait_send()
        return carry

    lax.fori_loop(1, steps, drain, 0)

    def drain_stat(k, carry):
        stat_copy(k).wait_send()
        return carry

    lax.fori_loop(1, tiles, drain_stat, 0)
    for which_act in range(2):
        halo_up(which_act).wait_send()
        halo_down(which_act).wait_send()
    for row in range(2):
        onward(row).wait_send()


def per_device(
    spans, tiles, features, norm_gain, query_weight, key_weight, value_weight, out_weight, conv_weight, skip_weight
):
    frames, rows, cols, channels = features.shape
    out_channels = conv_weight.shape[-1]
    cells = rows * cols
    steps = tiles // 2
    anywhere = pl.BlockSpec(memory_space=pl.ANY)
    vmem = pl.BlockSpec(memory_space=pltpu.VMEM)
    dma = pltpu.SemaphoreType.DMA
    out = pl.pallas_call(
        functools.partial(kernel, spans, tiles),
        out_shape=jax.ShapeDtypeStruct((2, cells, out_channels), BF16),
        in_specs=[anywhere, vmem] + [anywhere] * 6,
        out_specs=vmem,
        scratch_shapes=[
            pltpu.VMEM((steps, 4, cols, channels), BF16),
            pltpu.VMEM((cells, channels), BF16),
            pltpu.VMEM((cells, channels), F32),
            pltpu.VMEM((cells, 128), F32),
            pltpu.VMEM((cells, 128), F32),
            pltpu.VMEM((tiles, 1, 128), F32),
            pltpu.VMEM((cells, channels), BF16),
            pltpu.VMEM((2, 4, cols, channels), BF16),
            pltpu.VMEM((cells, out_channels), F32),
            pltpu.VMEM((cells, out_channels), F32),
            pltpu.VMEM((8, channels), F32),
            pltpu.VMEM((channels, channels), BF16),
            pltpu.VMEM((channels, channels), BF16),
            pltpu.VMEM((channels, channels), BF16),
            pltpu.VMEM((channels, channels), BF16),
            pltpu.VMEM((3, 3, channels, 3 * out_channels), BF16),
            pltpu.VMEM((channels, out_channels), BF16),
            dma((steps, 2)), dma((steps, 2)), dma((steps,)), dma((steps,)),
            dma((tiles,)), dma((tiles,)), dma((6,)), dma((6,)), dma((6,)), dma((27,)),
        ],
        compiler_params=pltpu.CompilerParams(
            collective_id=0, has_side_effects=True, vmem_limit_bytes=50 * 1024 * 1024
        ),
        name="mid_block_decode",
    )(
        features.reshape(rows, cols, channels), norm_gain.reshape(1, channels),
        query_weight, key_weight, value_weight, out_weight, conv_weight, skip_weight,
    )
    return out.reshape(2 * frames, rows, cols, out_channels)


def solution(mesh):
    spans, tiles = mesh.shape["tm"], mesh.shape["tile"]
    in_specs = (P("tm", "tile", None, None), P(), P(), P(), P(), P(), P(), P())
    return jax.shard_map(
        functools.partial(per_device, spans, tiles), mesh=mesh, in_specs=in_specs,
        out_specs=P("tm", "tile", None, None), check_vma=False,
    )
```

```python
import functools
import math

import jax
import jax.numpy as jnp
from jax import lax
from jax.experimental import pallas as pl
from jax.experimental.pallas import tpu as pltpu
from jax.sharding import PartitionSpec as P

GROUPS = 32
EPS = 1e-06
MESH = pl.DeviceIdType.MESH
F32 = jnp.float32
BF16 = jnp.bfloat16


def group_sum(v, width):
    lanes = v.shape[-1]
    lane = lax.broadcasted_iota(jnp.int32, v.shape, 1)
    step = 1
    while step < width:
        above = pltpu.roll(v, lanes - step, 1)
        below = pltpu.roll(v, step, 1)
        v = v + jnp.where((lane & step) == 0, above, below)
        step *= 2
    return v


def kernel(
    spans, tiles, x_hbm, gain_ref, wq_hbm, wk_hbm, wv_hbm, wo_hbm, wc_hbm, ws_hbm,
    out_ref,
    slots, q2, acc, peak, total, stats, mid, act, even, odd, ab,
    wq, wk, wv, wo, wc, ws,
    ring_send, ring_recv, sib_send, sib_recv, st_send, st_recv, edge_send, edge_recv, load_sem, conv_sem,
):
    rows, cols, channels = x_hbm.shape
    cells = rows * cols
    out_channels = ws.shape[1]
    width = channels // GROUPS
    blocks = channels // 128
    chips = tiles // 2
    steps = chips

    t = lax.axis_index("tm")
    i = lax.axis_index("tile")
    y = i // 2
    core = i - 2 * y
    right = lax.rem(i + 2, tiles)
    left = lax.rem(i + tiles - 2, tiles)
    sibling = 2 * y + 1 - core
    above = lax.rem(i + tiles - 1, tiles)
    below = lax.rem(i + 1, tiles)
    t_next = lax.rem(t + 1, spans)
    t_prev = lax.rem(t + spans - 1, spans)

    def remote(src, dst, send, recv, where):
        return pltpu.make_async_remote_copy(
            src_ref=src, dst_ref=dst, send_sem=send, recv_sem=recv, device_id=where, device_id_type=MESH
        )

    loads = [
        pltpu.make_async_copy(x_hbm, slots.at[0, pl.ds(0, 2)], load_sem.at[0]),
        pltpu.make_async_copy(wq_hbm, wq, load_sem.at[1]),
        pltpu.make_async_copy(wk_hbm, wk, load_sem.at[2]),
        pltpu.make_async_copy(wv_hbm, wv, load_sem.at[3]),
        pltpu.make_async_copy(wo_hbm, wo, load_sem.at[4]),
        pltpu.make_async_copy(ws_hbm, ws, load_sem.at[5]),
    ]
    loads[0].start()

    barrier = pltpu.get_barrier_semaphore()

    def greet(k, carry):
        pl.semaphore_signal(barrier, inc=1, device_id=(t, lax.rem(i + k, tiles)), device_id_type=MESH)
        return carry

    lax.fori_loop(1, tiles, greet, 0)
    has_next = t < spans - 1
    has_prev = t > 0

    @pl.when(has_next)
    def _():
        pl.semaphore_signal(barrier, inc=1, device_id=(t_next, i), device_id_type=MESH)

    @pl.when(has_prev)
    def _():
        pl.semaphore_signal(barrier, inc=1, device_id=(t_prev, i), device_id_type=MESH)

    pl.semaphore_wait(barrier, tiles - 1 + jnp.where(has_next, 1, 0) + jnp.where(has_prev, 1, 0))

    def first(h, lane):
        row = h if lane == 0 else 1 - h
        return remote(
            x_hbm.at[row], slots.at[1 + h, lane], ring_send.at[1 + h, lane], ring_recv.at[1 + h, lane],
            (t, right if lane == 0 else left),
        )

    for lane in range(2):
        first(0, lane).start()
    own_to_sibling = remote(
        x_hbm, slots.at[0, pl.ds(2, 2)], sib_send.at[0], sib_recv.at[0], (t, sibling)
    )
    own_to_sibling.start()

    def load_tap(k, carry):
        dt = k // 9
        dy = (k - 9 * dt) // 3
        dx = k - 9 * dt - 3 * dy
        column = pl.multiple_of(dt * out_channels, out_channels)
        pltpu.make_async_copy(
            wc_hbm.at[dt, dy, dx], wc.at[dx, dy, :, pl.ds(column, out_channels)], conv_sem.at[k]
        ).start()
        return carry

    loads[0].wait()
    own = slots[0, 0:2].reshape(cells, channels).astype(F32)
    sums = jnp.sum(own, axis=0, keepdims=True)
    squares = jnp.sum(own * own, axis=0, keepdims=True)
    sums = group_sum(jnp.broadcast_to(sums, (8, channels)), width)
    squares = group_sum(jnp.broadcast_to(squares, (8, channels)), width)
    lane_of = lax.broadcasted_iota(jnp.int32, (8, 128), 1) & (width - 1)
    packed = jnp.zeros((8, 128), F32)
    for k in range(2 * blocks):
        source = sums if k < blocks else squares
        b = k % blocks
        packed = jnp.where(lane_of == k, source[:, b * 128:(b + 1) * 128], packed)
    stats[0] = packed[0:1]

    def stat_copy(k):
        return remote(
            stats.at[0], stats.at[k], st_send.at[k], st_recv.at[k], (t, lax.rem(i + k, tiles))
        )

    def send_stat(k, carry):
        stat_copy(k).start()
        return carry

    lax.fori_loop(1, tiles, send_stat, 0)
    for lane in range(2):
        first(1, lane).start()
    for copy in loads[1:]:
        copy.start()

    def ring_copy(e, lane):
        return remote(
            slots.at[e, lane], slots.at[e + 2, lane], ring_send.at[e + 2, lane], ring_recv.at[e + 2, lane],
            (t, right if lane == 0 else left),
        )

    def ring_arrival(e, lane):
        return remote(
            slots.at[e, lane], slots.at[e, lane], ring_send.at[e, lane], ring_recv.at[e, lane],
            (t, right if lane == 0 else left),
        )

    def sib_copy(e):
        return remote(
            slots.at[e, pl.ds(0, 2)], slots.at[e, pl.ds(2, 2)], sib_send.at[e], sib_recv.at[e], (t, sibling)
        )

    def prepare():
        def take(k, carry):
            stat_copy(k).wait_recv()
            return carry

        lax.fori_loop(1, tiles, take, 0)
        whole = stats[0]
        for k in range(1, tiles):
            whole = whole + stats[k]
        whole = jnp.broadcast_to(whole, (8, 128))
        spread = [group_sum(jnp.where(lane_of == k, whole, 0.0), width) for k in range(2 * blocks)]
        population = float(tiles * cells * width)
        mean = jnp.concatenate(spread[:blocks], axis=1)[0:1] / population
        var = jnp.concatenate(spread[blocks:], axis=1)[0:1] / population - mean * mean
        rstd = lax.rsqrt(var + EPS)
        gain = gain_ref[...]
        ab[0:1] = rstd * gain
        ab[1:2] = -mean * rstd * gain
        block = slots[0, 0:2].reshape(cells, channels).astype(F32)
        normed = (((block - mean) * rstd) * gain).astype(BF16)
        loads[1].wait()
        queries = jnp.dot(normed, wq[...], preferred_element_type=F32).astype(BF16)
        loads[2].wait()
        inner = lax.dot_general(queries, wk[...], (((1,), (1,)), ((), ())), preferred_element_type=F32)
        scale = channels ** (-0.5) * math.log2(math.e)
        q2[...] = (inner * (rstd * gain * scale)).astype(BF16)
        acc[...] = jnp.zeros_like(acc)
        total[...] = jnp.zeros_like(total)
        peak[...] = jnp.full_like(peak, -jnp.inf)

    def attend(e):
        keys = slots[e].reshape(4 * cols, channels)
        scores = lax.dot_general(q2[...], keys, (((1,), (1,)), ((), ())), preferred_element_type=F32)
        before = peak[:, 0:1]
        now = jnp.maximum(before, jnp.max(scores, axis=1, keepdims=True))
        fade = jnp.exp2(before - now)
        weights = jnp.exp2(scores - now).astype(BF16)
        peak[...] = jnp.broadcast_to(now, peak.shape)
        total[...] = total[...] * fade + jnp.sum(weights.astype(F32), axis=1, keepdims=True)
        acc[...] = acc[...] * fade + jnp.dot(weights, keys, preferred_element_type=F32)

    def arrive(e):
        for lane in range(2):
            ring_arrival(e, lane).wait_recv()

            @pl.when(e < steps - 2)
            def _():
                ring_copy(e, lane).start()

        sib_copy(e).start()

    def attend_step(e, carry):
        sib_copy(e).wait_recv()
        attend(e)
        return carry

    def gather_step(e, carry):
        @pl.when(e < steps)
        def _():
            arrive(e)

        @pl.when(e == 2)
        def _():
            prepare()

        @pl.when(e == 3)
        def _():
            lax.fori_loop(0, 27, load_tap, 0)

        low = jnp.where(e == 3, 1, e - 1)
        low = jnp.where(e == 2, 0, low)
        high = jnp.where(e == 2, 1, e)
        high = jnp.where(e == 1, low, high)
        lax.fori_loop(low, high, attend_step, 0)
        return carry

    lax.fori_loop(1, steps + 1, gather_step, 0)

    loads[3].wait()
    loads[4].wait()

    def halo_up(which):
        return remote(
            act.at[which, 1], act.at[which, 3], edge_send.at[2 * which], edge_recv.at[2 * which], (t, above)
        )

    def halo_down(which):
        return remote(
            act.at[which, 2], act.at[which, 0], edge_send.at[2 * which + 1], edge_recv.at[2 * which + 1], (t, below)
        )

    def onward(row):
        return remote(
            act.at[0, 1 + row], act.at[1, 1 + row], edge_send.at[4 + row], edge_recv.at[4 + row], (t_next, i)
        )

    def finish(k, carry):
        row = k + core - 2 * k * core
        part = pl.ds(pl.multiple_of(row * cols, cols), cols)
        mixed = acc[part, :] * (1.0 / total[part, 0:1])
        mixed = (mixed * ab[0:1] + ab[1:2]).astype(BF16)
        attended = jnp.dot(mixed, wv[...], preferred_element_type=F32).astype(BF16)
        change = jnp.dot(attended, wo[...], preferred_element_type=F32)
        mid_row = (slots[0, row].astype(F32) + change).astype(BF16)
        mid[part, :] = mid_row
        wide = mid_row.astype(F32)
        act[0, 1 + row] = (wide * (1.0 / (1.0 + jnp.exp(-wide)))).astype(BF16)

        @pl.when(has_next)
        def _():
            onward(row).start()

        @pl.when(row == 0)
        def _():
            halo_up(0).start()

        @pl.when(row == 1)
        def _():
            halo_down(0).start()

        return carry

    lax.fori_loop(0, 2, finish, 0)

    loads[5].wait()

    def tap_wait(k, carry):
        dt = k // 9
        dy = (k - 9 * dt) // 3
        dx = k - 9 * dt - 3 * dy
        column = pl.multiple_of(dt * out_channels, out_channels)
        pltpu.make_async_copy(
            wc_hbm.at[dt, dy, dx], wc.at[dx, dy, :, pl.ds(column, out_channels)], conv_sem.at[k]
        ).wait()
        return carry

    lax.fori_loop(0, 27, tap_wait, 0)
    skip = jnp.dot(mid[...], ws[...], preferred_element_type=F32)
    even[...] = skip
    odd[...] = skip
    position = lax.rem(lax.broadcasted_iota(jnp.int32, (cells, 1), 0), cols)

    def product(which, dx, start):
        z = None
        for dy in range(3):
            piece = act[which, dy:dy + 2].reshape(cells, channels)
            part = jnp.dot(piece, wc[dx, dy, :, start:start + 2 * out_channels], preferred_element_type=F32)
            z = part if z is None else z + part
        if dx == 0:
            z = jnp.where(position == 0, 0.0, pltpu.roll(z, 1, 0))
        if dx == 2:
            z = jnp.where(position == cols - 1, 0.0, pltpu.roll(z, cells - 1, 0))
        return z[:, :out_channels], z[:, out_channels:]

    def clear(which):
        @pl.when(i == 0)
        def _():
            act[which, 0] = jnp.zeros((cols, channels), BF16)

        @pl.when(i == tiles - 1)
        def _():
            act[which, 3] = jnp.zeros((cols, channels), BF16)

    halo_up(0).wait_recv()
    halo_down(0).wait_recv()
    clear(0)
    for dx in range(3):
        second, third = product(0, dx, out_channels)
        even[...] += third
        odd[...] += second + third

    def pass_on(k, carry):
        row = k + core - 2 * k * core
        onward(row).wait_recv()

        @pl.when(row == 0)
        def _():
            halo_up(1).start()

        @pl.when(row == 1)
        def _():
            halo_down(1).start()

        return carry

    @pl.when(has_prev)
    def _():
        lax.fori_loop(0, 2, pass_on, 0)
        halo_up(1).wait_recv()
        halo_down(1).wait_recv()
        clear(1)

    which = jnp.where(t == 0, 0, 1)
    for dx in range(3):
        one, second = product(which, dx, 0)
        even[...] += one + second
        odd[...] += one
    out_ref[0] = even[...].astype(BF16)
    out_ref[1] = odd[...].astype(BF16)

    for h in range(2):
        for lane in range(2):
            first(h, lane).wait_send()
    own_to_sibling.wait_send()

    def drain(e, carry):
        for lane in range(2):
            @pl.when(e < steps - 2)
            def _():
                ring_copy(e, lane).wait_send()
        sib_copy(e).wait_send()
        return carry

    lax.fori_loop(1, steps, drain, 0)

    def drain_stat(k, carry):
        stat_copy(k).wait_send()
        return carry

    lax.fori_loop(1, tiles, drain_stat, 0)
    halo_up(0).wait_send()
    halo_down(0).wait_send()

    @pl.when(has_prev)
    def _():
        halo_up(1).wait_send()
        halo_down(1).wait_send()

    @pl.when(has_next)
    def _():
        for row in range(2):
            onward(row).wait_send()


def per_device(
    spans, tiles, features, norm_gain, query_weight, key_weight, value_weight, out_weight, conv_weight, skip_weight
):
    frames, rows, cols, channels = features.shape
    out_channels = conv_weight.shape[-1]
    cells = rows * cols
    steps = tiles // 2
    anywhere = pl.BlockSpec(memory_space=pl.ANY)
    vmem = pl.BlockSpec(memory_space=pltpu.VMEM)
    dma = pltpu.SemaphoreType.DMA
    out = pl.pallas_call(
        functools.partial(kernel, spans, tiles),
        out_shape=jax.ShapeDtypeStruct((2, cells, out_channels), BF16),
        in_specs=[anywhere, vmem] + [anywhere] * 6,
        out_specs=vmem,
        scratch_shapes=[
            pltpu.VMEM((steps, 4, cols, channels), BF16),
            pltpu.VMEM((cells, channels), BF16),
            pltpu.VMEM((cells, channels), F32),
            pltpu.VMEM((cells, 128), F32),
            pltpu.VMEM((cells, 128), F32),
            pltpu.VMEM((tiles, 1, 128), F32),
            pltpu.VMEM((cells, channels), BF16),
            pltpu.VMEM((2, 4, cols, channels), BF16),
            pltpu.VMEM((cells, out_channels), F32),
            pltpu.VMEM((cells, out_channels), F32),
            pltpu.VMEM((8, channels), F32),
            pltpu.VMEM((channels, channels), BF16),
            pltpu.VMEM((channels, channels), BF16),
            pltpu.VMEM((channels, channels), BF16),
            pltpu.VMEM((channels, channels), BF16),
            pltpu.VMEM((3, 3, channels, 3 * out_channels), BF16),
            pltpu.VMEM((channels, out_channels), BF16),
            dma((steps, 2)), dma((steps, 2)), dma((steps,)), dma((steps,)),
            dma((tiles,)), dma((tiles,)), dma((6,)), dma((6,)), dma((6,)), dma((27,)),
        ],
        compiler_params=pltpu.CompilerParams(
            collective_id=0, has_side_effects=True, vmem_limit_bytes=62 * 1024 * 1024
        ),
        name="mid_block_decode",
    )(
        features.reshape(rows, cols, channels), norm_gain.reshape(1, channels),
        query_weight, key_weight, value_weight, out_weight, conv_weight, skip_weight,
    )
    return out.reshape(2 * frames, rows, cols, out_channels)


def solution(mesh):
    spans, tiles = mesh.shape["tm"], mesh.shape["tile"]
    in_specs = (P("tm", "tile", None, None), P(), P(), P(), P(), P(), P(), P())
    return jax.shard_map(
        functools.partial(per_device, spans, tiles), mesh=mesh, in_specs=in_specs,
        out_specs=P("tm", "tile", None, None), check_vma=False,
    )
```

```python
import functools
import math

import jax
import jax.numpy as jnp
from jax import lax
from jax.experimental import pallas as pl
from jax.experimental.pallas import tpu as pltpu
from jax.sharding import PartitionSpec as P

GROUPS = 32
EPS = 1e-06
MESH = pl.DeviceIdType.MESH
F32 = jnp.float32
BF16 = jnp.bfloat16


def group_sum(v, width):
    lanes = v.shape[-1]
    lane = lax.broadcasted_iota(jnp.int32, v.shape, 1)
    step = 1
    while step < width:
        above = pltpu.roll(v, lanes - step, 1)
        below = pltpu.roll(v, step, 1)
        v = v + jnp.where((lane & step) == 0, above, below)
        step *= 2
    return v


def remote(src, dst, send, recv, where):
    return pltpu.make_async_remote_copy(
        src_ref=src, dst_ref=dst, send_sem=send, recv_sem=recv, device_id=where, device_id_type=MESH
    )


def kernel(
    spans, tiles, x_hbm, gain_hbm, wq_hbm, wk_hbm, wv_hbm, wo_hbm, wc_hbm, ws_hbm, out_ref,
    slots, q2, acc, peak, total, stats, ab, gain, wq, wk, wv, wo, ws,
    act, mid, near, far, base, wc,
    ring_send, ring_recv, sib_send, sib_recv, st_send, st_recv, load_sem, edge_send, edge_recv, conv_sem,
):
    rows, cols, channels = x_hbm.shape
    outs = ws.shape[1]
    cells = rows * cols
    width = channels // GROUPS
    blocks = channels // 128
    steps = tiles // 2

    t = lax.axis_index("tm")
    i = lax.axis_index("tile")
    y = i // 2
    core = i - 2 * y
    right = lax.rem(i + 2, tiles)
    left = lax.rem(i + tiles - 2, tiles)
    sibling = 2 * y + 1 - core
    above = lax.rem(i + tiles - 1, tiles)
    below = lax.rem(i + 1, tiles)
    t_next = lax.rem(t + 1, spans)
    t_prev = lax.rem(t + spans - 1, spans)
    has_next = t < spans - 1
    has_prev = t > 0

    loads = [
        pltpu.make_async_copy(x_hbm, slots.at[0, pl.ds(0, 2)], load_sem.at[0]),
        pltpu.make_async_copy(wq_hbm, wq, load_sem.at[1]),
        pltpu.make_async_copy(wk_hbm, wk, load_sem.at[2]),
        pltpu.make_async_copy(gain_hbm, gain, load_sem.at[3]),
        pltpu.make_async_copy(wv_hbm, wv, load_sem.at[4]),
        pltpu.make_async_copy(wo_hbm, wo, load_sem.at[5]),
        pltpu.make_async_copy(ws_hbm, ws, load_sem.at[6]),
    ]
    loads[0].start()

    barrier = pltpu.get_barrier_semaphore()

    def greet(k, carry):
        pl.semaphore_signal(barrier, inc=1, device_id=(t, lax.rem(i + k, tiles)), device_id_type=MESH)
        return carry

    lax.fori_loop(1, tiles, greet, 0)

    @pl.when(has_prev)
    def _():
        pl.semaphore_signal(barrier, inc=1, device_id=(t_prev, i), device_id_type=MESH)

    pl.semaphore_wait(barrier, tiles - 1 + jnp.where(has_next, 1, 0))

    def first(h, lane):
        row = h if lane == 0 else 1 - h
        return remote(
            x_hbm.at[row], slots.at[1 + h, lane], ring_send.at[1 + h, lane], ring_recv.at[1 + h, lane],
            (t, right if lane == 0 else left),
        )

    for lane in range(2):
        first(0, lane).start()
    own_to_sibling = remote(
        x_hbm, slots.at[0, pl.ds(2, 2)], sib_send.at[0], sib_recv.at[0], (t, sibling)
    )
    own_to_sibling.start()

    loads[0].wait()
    own = slots[0, 0:2].reshape(cells, channels).astype(F32)
    sums = jnp.sum(own, axis=0, keepdims=True)
    squares = jnp.sum(own * own, axis=0, keepdims=True)
    sums = group_sum(jnp.broadcast_to(sums, (8, channels)), width)
    squares = group_sum(jnp.broadcast_to(squares, (8, channels)), width)
    lane_of = lax.broadcasted_iota(jnp.int32, (8, 128), 1) & (width - 1)
    packed = jnp.zeros((8, 128), F32)
    for k in range(2 * blocks):
        source = sums if k < blocks else squares
        b = k % blocks
        packed = jnp.where(lane_of == k, source[:, b * 128:(b + 1) * 128], packed)
    stats[0] = packed[0:1]

    def stat_copy(k):
        return remote(
            stats.at[0], stats.at[k], st_send.at[k], st_recv.at[k], (t, lax.rem(i + k, tiles))
        )

    def send_stat(k, carry):
        stat_copy(k).start()
        return carry

    lax.fori_loop(1, tiles, send_stat, 0)
    for lane in range(2):
        first(1, lane).start()
    for copy in loads[1:]:
        copy.start()

    def ring_copy(e, lane):
        return remote(
            slots.at[e, lane], slots.at[e + 2, lane], ring_send.at[e + 2, lane], ring_recv.at[e + 2, lane],
            (t, right if lane == 0 else left),
        )

    def ring_arrival(e, lane):
        return remote(
            slots.at[e, lane], slots.at[e, lane], ring_send.at[e, lane], ring_recv.at[e, lane],
            (t, right if lane == 0 else left),
        )

    def sib_copy(e):
        return remote(
            slots.at[e, pl.ds(0, 2)], slots.at[e, pl.ds(2, 2)], sib_send.at[e], sib_recv.at[e], (t, sibling)
        )

    def prepare():
        def take(k, carry):
            stat_copy(k).wait_recv()
            return carry

        lax.fori_loop(1, tiles, take, 0)
        whole = stats[0]
        for k in range(1, tiles):
            whole = whole + stats[k]
        whole = jnp.broadcast_to(whole, (8, 128))
        spread = [group_sum(jnp.where(lane_of == k, whole, 0.0), width) for k in range(2 * blocks)]
        population = float(tiles * cells * width)
        mean = jnp.concatenate(spread[:blocks], axis=1)[0:1] / population
        var = jnp.concatenate(spread[blocks:], axis=1)[0:1] / population - mean * mean
        rstd = lax.rsqrt(var + EPS)
        loads[3].wait()
        scaled = rstd * gain[...]
        ab[0:1] = scaled
        ab[1:2] = -mean * scaled
        block = slots[0, 0:2].reshape(cells, channels).astype(F32)
        normed = (((block - mean) * rstd) * gain[...]).astype(BF16)
        loads[1].wait()
        queries = jnp.dot(normed, wq[...], preferred_element_type=F32).astype(BF16)
        loads[2].wait()
        inner = lax.dot_general(queries, wk[...], (((1,), (1,)), ((), ())), preferred_element_type=F32)
        scale = channels ** (-0.5) * math.log2(math.e)
        q2[...] = (inner * (scaled * scale)).astype(BF16)
        acc[...] = jnp.zeros_like(acc)
        total[...] = jnp.zeros_like(total)
        peak[...] = jnp.full_like(peak, -jnp.inf)

    def attend(e):
        keys = slots[e].reshape(4 * cols, channels)
        scores = lax.dot_general(q2[...], keys, (((1,), (1,)), ((), ())), preferred_element_type=F32)
        before = peak[:, 0:1]
        now = jnp.maximum(before, jnp.max(scores, axis=1, keepdims=True))
        fade = jnp.exp2(before - now)
        weights = jnp.exp2(scores - now).astype(BF16)
        peak[...] = jnp.broadcast_to(now, peak.shape)
        total[...] = total[...] * fade + jnp.sum(weights.astype(F32), axis=1, keepdims=True)
        acc[...] = acc[...] * fade + jnp.dot(weights, keys, preferred_element_type=F32)

    def arrive(e):
        for lane in range(2):
            ring_arrival(e, lane).wait_recv()

            @pl.when(e < steps - 2)
            def _():
                ring_copy(e, lane).start()

        sib_copy(e).start()

    def attend_step(e, carry):
        sib_copy(e).wait_recv()
        attend(e)
        return carry

    def tap(k):
        dt = k // 9
        dy = (k - 9 * dt) // 3
        dx = k - 9 * dt - 3 * dy
        column = pl.multiple_of(dt * outs, outs)
        return pltpu.make_async_copy(wc_hbm.at[dt, dy, dx], wc.at[dx, dy, :, pl.ds(column, outs)], conv_sem.at[k])

    def load_tap(k, carry):
        tap(k).start()
        return carry

    def take_tap(k, carry):
        tap(k).wait()
        return carry

    def gather_step(e, carry):
        @pl.when(e < steps)
        def _():
            arrive(e)

        @pl.when(e == 2)
        def _():
            prepare()

        @pl.when(e == 3)
        def _():
            lax.fori_loop(0, 27, load_tap, 0)

        low = jnp.where(e == 3, 1, e - 1)
        low = jnp.where(e == 2, 0, low)
        high = jnp.where(e == 2, 1, e)
        high = jnp.where(e == 1, low, high)
        lax.fori_loop(low, high, attend_step, 0)
        return carry

    lax.fori_loop(1, steps + 1, gather_step, 0)

    def halo_up(which):
        return remote(
            act.at[which, 1], act.at[which, 3], edge_send.at[2 * which], edge_recv.at[2 * which], (t, above)
        )

    def halo_down(which):
        return remote(
            act.at[which, 2], act.at[which, 0], edge_send.at[2 * which + 1], edge_recv.at[2 * which + 1], (t, below)
        )

    def onward(row):
        return remote(
            act.at[0, 1 + row], act.at[1, 1 + row], edge_send.at[4 + row], edge_recv.at[4 + row], (t_next, i)
        )

    def send_halo(which, row):
        @pl.when(row == 0)
        def _():
            halo_up(which).start()

        @pl.when(row == 1)
        def _():
            halo_down(which).start()

    loads[4].wait()
    loads[5].wait()

    def finish(k, carry):
        row = k + core - 2 * k * core
        part = pl.ds(pl.multiple_of(row * cols, cols), cols)
        mixed = (acc[part, :] * (1.0 / total[part, 0:1]) * ab[0:1] + ab[1:2]).astype(BF16)
        attended = jnp.dot(mixed, wv[...], preferred_element_type=F32).astype(BF16)
        change = jnp.dot(attended, wo[...], preferred_element_type=F32)
        mid_row = (slots[0, row].astype(F32) + change).astype(BF16)
        mid[part, :] = mid_row
        wide = mid_row.astype(F32)
        act[0, 1 + row] = (wide * (1.0 / (1.0 + jnp.exp(-wide)))).astype(BF16)

        @pl.when(has_next)
        def _():
            onward(row).start()

        send_halo(0, row)
        return carry

    lax.fori_loop(0, 2, finish, 0)

    loads[6].wait()
    skip = jnp.dot(mid[...], ws[...], preferred_element_type=F32)
    base[:, :outs] = skip
    base[:, outs:] = skip
    near[...] = jnp.zeros_like(near)
    far[...] = jnp.zeros_like(far)
    lax.fori_loop(0, 27, take_tap, 0)

    def visit(n):
        own = n < 4
        first = lax.rem(n, 2) == 0
        inner = n // 2
        mine = jnp.where(inner == 0, 1 + core, 2 - core)
        halo = jnp.where(first, 3 * core, 3 - 3 * core)
        source = jnp.where(own, mine, halo)
        same = jnp.where(inner == 0, core, 1 - core)
        target = jnp.where(own, jnp.where(first, same, 1 - same), jnp.where(first, core, 1 - core))
        return source, target, source - target

    def add_row(sums, which, n, start):
        source, target, dy = visit(n)
        row = act[which, source]
        part = pl.ds(pl.multiple_of(target * cols, cols), cols)
        for dx in range(3):
            sums[dx, part, :] += jnp.dot(row, wc[dx, dy, :, start:start + 2 * outs], preferred_element_type=F32)

    position = lax.rem(lax.broadcasted_iota(jnp.int32, (cells, 1), 0), cols)

    def shifted(z, dx):
        if dx == 0:
            return jnp.where(position == 0, 0.0, pltpu.roll(z, 1, 0))
        if dx == 2:
            return jnp.where(position == cols - 1, 0.0, pltpu.roll(z, cells - 1, 0))
        return z

    at_rim = jnp.where(core == 0, i == 0, i == tiles - 1)

    def near_step(n, carry):
        @pl.when(n == 4)
        def _():
            halo_up(0).wait_recv()
            halo_down(0).wait_recv()

        @pl.when(jnp.logical_not(jnp.logical_and(n == 4, at_rim)))
        def _():
            add_row(near, 0, n, outs)

        return carry

    lax.fori_loop(0, 6, near_step, 0)
    for dx in range(3):
        z = shifted(near[dx], dx)
        base[:, :outs] += z[:, outs:]
        base[:, outs:] += z[:, :outs] + z[:, outs:]

    which = jnp.where(t == 0, 0, 1)

    def far_step(n, carry):
        @pl.when(jnp.logical_and(has_prev, jnp.logical_or(n == 0, n == 2)))
        def _():
            row = jnp.where(n == 0, core, 1 - core)
            onward(row).wait_recv()
            send_halo(1, row)

        @pl.when(jnp.logical_and(has_prev, n == 4))
        def _():
            @pl.when(core == 0)
            def _():
                halo_down(1).wait_recv()

            @pl.when(core == 1)
            def _():
                halo_up(1).wait_recv()

        @pl.when(jnp.logical_and(has_prev, n == 5))
        def _():
            @pl.when(core == 0)
            def _():
                halo_up(1).wait_recv()

            @pl.when(core == 1)
            def _():
                halo_down(1).wait_recv()

        @pl.when(jnp.logical_not(jnp.logical_and(n == 4, at_rim)))
        def _():
            add_row(far, which, n, 0)

        return carry

    lax.fori_loop(0, 6, far_step, 0)
    even = base[:, :outs]
    odd = base[:, outs:]
    for dx in range(3):
        z = shifted(far[dx], dx)
        even = even + (z[:, :outs] + z[:, outs:])
        odd = odd + z[:, :outs]
    out_ref[0] = even.astype(BF16)
    out_ref[1] = odd.astype(BF16)

    for h in range(2):
        for lane in range(2):
            first(h, lane).wait_send()
    own_to_sibling.wait_send()

    def drain(e, carry):
        for lane in range(2):
            @pl.when(e < steps - 2)
            def _():
                ring_copy(e, lane).wait_send()
        sib_copy(e).wait_send()
        return carry

    lax.fori_loop(1, steps, drain, 0)

    def drain_stat(k, carry):
        stat_copy(k).wait_send()
        return carry

    lax.fori_loop(1, tiles, drain_stat, 0)
    halo_up(0).wait_send()
    halo_down(0).wait_send()

    @pl.when(has_prev)
    def _():
        halo_up(1).wait_send()
        halo_down(1).wait_send()

    @pl.when(has_next)
    def _():
        for row in range(2):
            onward(row).wait_send()


def per_device(
    spans, tiles, features, norm_gain, query_weight, key_weight, value_weight, out_weight, conv_weight, skip_weight
):
    frames, rows, cols, channels = features.shape
    outs = conv_weight.shape[-1]
    cells = rows * cols
    steps = tiles // 2
    hbm = pl.BlockSpec(memory_space=pltpu.HBM)
    dma = pltpu.SemaphoreType.DMA
    operands = (
        features.reshape(rows, cols, channels), norm_gain.reshape(1, channels),
        query_weight, key_weight, value_weight, out_weight, conv_weight, skip_weight,
    )
    operands = [pltpu.with_memory_space_constraint(operand, pltpu.HBM) for operand in operands]
    out = pl.pallas_call(
        functools.partial(kernel, spans, tiles),
        out_shape=jax.ShapeDtypeStruct((2, cells, outs), BF16),
        in_specs=[hbm] * 8,
        out_specs=pl.BlockSpec(memory_space=pltpu.VMEM),
        scratch_shapes=[
            pltpu.VMEM((steps, 4, cols, channels), BF16),
            pltpu.VMEM((cells, channels), BF16),
            pltpu.VMEM((cells, channels), F32),
            pltpu.VMEM((cells, 128), F32),
            pltpu.VMEM((cells, 128), F32),
            pltpu.VMEM((tiles, 1, 128), F32),
            pltpu.VMEM((8, channels), F32),
            pltpu.VMEM((1, channels), F32),
            pltpu.VMEM((channels, channels), BF16),
            pltpu.VMEM((channels, channels), BF16),
            pltpu.VMEM((channels, channels), BF16),
            pltpu.VMEM((channels, channels), BF16),
            pltpu.VMEM((channels, outs), BF16),
            pltpu.VMEM((2, 4, cols, channels), BF16),
            pltpu.VMEM((cells, channels), BF16),
            pltpu.VMEM((3, cells, 2 * outs), F32),
            pltpu.VMEM((3, cells, 2 * outs), F32),
            pltpu.VMEM((cells, 2 * outs), F32),
            pltpu.VMEM((3, 3, channels, 3 * outs), BF16),
            dma((steps, 2)), dma((steps, 2)), dma((steps,)), dma((steps,)), dma((tiles,)), dma((tiles,)), dma((7,)),
            dma((6,)), dma((6,)), dma((27,)),
        ],
        compiler_params=pltpu.CompilerParams(
            collective_id=0, has_side_effects=True, vmem_limit_bytes=50 * 1024 * 1024
        ),
        name="mid_block_decode",
    )(*operands)
    return out.reshape(2 * frames, rows, cols, outs)


def solution(mesh):
    spans, tiles = mesh.shape["tm"], mesh.shape["tile"]
    in_specs = (P("tm", "tile", None, None), P(), P(), P(), P(), P(), P(), P())
    return jax.shard_map(
        functools.partial(per_device, spans, tiles), mesh=mesh, in_specs=in_specs,
        out_specs=P("tm", "tile", None, None), check_vma=False,
    )
```

```python
import functools
import math

import jax
import jax.numpy as jnp
from jax import lax
from jax.experimental import pallas as pl
from jax.experimental.pallas import tpu as pltpu
from jax.sharding import PartitionSpec as P

GROUPS = 32
EPS = 1e-06
MESH = pl.DeviceIdType.MESH
F32 = jnp.float32
BF16 = jnp.bfloat16


def group_sum(v, width):
    lanes = v.shape[-1]
    lane = lax.broadcasted_iota(jnp.int32, v.shape, 1)
    step = 1
    while step < width:
        above = pltpu.roll(v, lanes - step, 1)
        below = pltpu.roll(v, step, 1)
        v = v + jnp.where((lane & step) == 0, above, below)
        step *= 2
    return v


def remote(src, dst, send, recv, where):
    return pltpu.make_async_remote_copy(
        src_ref=src, dst_ref=dst, send_sem=send, recv_sem=recv, device_id=where, device_id_type=MESH
    )


def kernel(
    spans, tiles, x_hbm, gain_hbm, wq_hbm, wk_hbm, wv_hbm, wo_hbm, wc_hbm, ws_hbm, out_ref,
    slots, q2, acc, peak, total, stats, ab, gain, wq, wk, wv, wo, wvo, ws,
    act, mid, near, far, base, wc,
    ring_send, ring_recv, sib_send, sib_recv, st_send, st_recv, load_sem, edge_send, edge_recv, conv_sem,
):
    rows, cols, channels = x_hbm.shape
    outs = ws.shape[1]
    cells = rows * cols
    width = channels // GROUPS
    blocks = channels // 128
    steps = tiles // 2

    t = lax.axis_index("tm")
    i = lax.axis_index("tile")
    y = i // 2
    core = i - 2 * y
    right = lax.rem(i + 2, tiles)
    left = lax.rem(i + tiles - 2, tiles)
    sibling = 2 * y + 1 - core
    above = lax.rem(i + tiles - 1, tiles)
    below = lax.rem(i + 1, tiles)
    t_next = lax.rem(t + 1, spans)
    t_prev = lax.rem(t + spans - 1, spans)
    has_next = t < spans - 1
    has_prev = t > 0

    loads = [
        pltpu.make_async_copy(x_hbm, slots.at[0, pl.ds(0, 2)], load_sem.at[0]),
        pltpu.make_async_copy(wq_hbm, wq, load_sem.at[1]),
        pltpu.make_async_copy(wk_hbm, wk, load_sem.at[2]),
        pltpu.make_async_copy(gain_hbm, gain, load_sem.at[3]),
        pltpu.make_async_copy(wv_hbm, wv, load_sem.at[4]),
        pltpu.make_async_copy(wo_hbm, wo, load_sem.at[5]),
        pltpu.make_async_copy(ws_hbm, ws, load_sem.at[6]),
    ]
    loads[0].start()

    barrier = pltpu.get_barrier_semaphore()

    def greet(k, carry):
        pl.semaphore_signal(barrier, inc=1, device_id=(t, lax.rem(i + k, tiles)), device_id_type=MESH)
        return carry

    lax.fori_loop(1, tiles, greet, 0)

    @pl.when(has_prev)
    def _():
        pl.semaphore_signal(barrier, inc=1, device_id=(t_prev, i), device_id_type=MESH)

    loads[0].wait()
    pl.semaphore_wait(barrier, tiles - 1 + jnp.where(has_next, 1, 0))

    def first(h, lane):
        row = h if lane == 0 else 1 - h
        return remote(
            slots.at[0, row], slots.at[1 + h, lane], ring_send.at[1 + h, lane], ring_recv.at[1 + h, lane],
            (t, right if lane == 0 else left),
        )

    for lane in range(2):
        first(0, lane).start()
    own_to_sibling = remote(
        slots.at[0, pl.ds(0, 2)], slots.at[0, pl.ds(2, 2)], sib_send.at[0], sib_recv.at[0], (t, sibling)
    )
    own_to_sibling.start()

    own = slots[0, 0:2].reshape(cells, channels).astype(F32)
    sums = jnp.sum(own, axis=0, keepdims=True)
    squares = jnp.sum(own * own, axis=0, keepdims=True)
    sums = group_sum(jnp.broadcast_to(sums, (8, channels)), width)
    squares = group_sum(jnp.broadcast_to(squares, (8, channels)), width)
    lane_of = lax.broadcasted_iota(jnp.int32, (8, 128), 1) & (width - 1)
    packed = jnp.zeros((8, 128), F32)
    for k in range(2 * blocks):
        source = sums if k < blocks else squares
        b = k % blocks
        packed = jnp.where(lane_of == k, source[:, b * 128:(b + 1) * 128], packed)
    stats[0] = packed[0:1]

    def stat_copy(k):
        return remote(
            stats.at[0], stats.at[k], st_send.at[k], st_recv.at[k], (t, lax.rem(i + k, tiles))
        )

    def send_stat(k, carry):
        stat_copy(k).start()
        return carry

    lax.fori_loop(1, tiles, send_stat, 0)
    for lane in range(2):
        first(1, lane).start()
    for copy in loads[1:]:
        copy.start()

    def ring_copy(e, lane):
        return remote(
            slots.at[e, lane], slots.at[e + 2, lane], ring_send.at[e + 2, lane], ring_recv.at[e + 2, lane],
            (t, right if lane == 0 else left),
        )

    def ring_arrival(e, lane):
        return remote(
            slots.at[e, lane], slots.at[e, lane], ring_send.at[e, lane], ring_recv.at[e, lane],
            (t, right if lane == 0 else left),
        )

    def sib_copy(e):
        return remote(
            slots.at[e, pl.ds(0, 2)], slots.at[e, pl.ds(2, 2)], sib_send.at[e], sib_recv.at[e], (t, sibling)
        )

    def prepare():
        def take(k, carry):
            stat_copy(k).wait_recv()
            return carry

        lax.fori_loop(1, tiles, take, 0)
        whole = stats[0]
        for k in range(1, tiles):
            whole = whole + stats[k]
        whole = jnp.broadcast_to(whole, (8, 128))
        spread = [group_sum(jnp.where(lane_of == k, whole, 0.0), width) for k in range(2 * blocks)]
        population = float(tiles * cells * width)
        mean = jnp.concatenate(spread[:blocks], axis=1)[0:1] / population
        var = jnp.concatenate(spread[blocks:], axis=1)[0:1] / population - mean * mean
        rstd = lax.rsqrt(var + EPS)
        loads[3].wait()
        scaled = rstd * gain[...]
        ab[0:1] = scaled
        ab[1:2] = -mean * scaled
        block = slots[0, 0:2].reshape(cells, channels).astype(F32)
        normed = (((block - mean) * rstd) * gain[...]).astype(BF16)
        loads[1].wait()
        queries = jnp.dot(normed, wq[...], preferred_element_type=F32).astype(BF16)
        loads[2].wait()
        inner = lax.dot_general(queries, wk[...], (((1,), (1,)), ((), ())), preferred_element_type=F32)
        scale = channels ** (-0.5) * math.log2(math.e)
        q2[...] = (inner * (scaled * scale)).astype(BF16)
        acc[...] = jnp.zeros_like(acc)
        total[...] = jnp.zeros_like(total)
        peak[...] = jnp.full_like(peak, -jnp.inf)

    def attend(e, begin, count):
        keys = slots[e, begin:begin + count].reshape(count * cols, channels)
        scores = lax.dot_general(q2[...], keys, (((1,), (1,)), ((), ())), preferred_element_type=F32)
        before = peak[:, 0:1]
        now = jnp.maximum(before, jnp.max(scores, axis=1, keepdims=True))
        fade = jnp.exp2(before - now)
        weights = jnp.exp2(scores - now).astype(BF16)
        peak[...] = jnp.broadcast_to(now, peak.shape)
        total[...] = total[...] * fade + jnp.sum(weights.astype(F32), axis=1, keepdims=True)
        acc[...] = acc[...] * fade + jnp.dot(weights, keys, preferred_element_type=F32)

    def arrive(e):
        for lane in range(2):
            ring_arrival(e, lane).wait_recv()

            @pl.when(e < steps - 2)
            def _():
                ring_copy(e, lane).start()

        sib_copy(e).start()

    def attend_step(e, carry):
        sib_copy(e).wait_recv()
        attend(e, 0, 4)
        return carry

    def tap(k):
        dt = k // 9
        dy = (k - 9 * dt) // 3
        dx = k - 9 * dt - 3 * dy
        column = pl.multiple_of(dt * outs, outs)
        return pltpu.make_async_copy(wc_hbm.at[dt, dy, dx], wc.at[dx, dy, :, pl.ds(column, outs)], conv_sem.at[k])

    def load_tap(k, carry):
        tap(k).start()
        return carry

    def take_tap(k, carry):
        tap(k).wait()
        return carry

    def tap(k):
        dt = k // 9
        dy = (k - 9 * dt) // 3
        dx = k - 9 * dt - 3 * dy
        column = pl.multiple_of(dt * outs, outs)
        return pltpu.make_async_copy(wc_hbm.at[dt, dy, dx], wc.at[dx, dy, :, pl.ds(column, outs)], conv_sem.at[k])

    def load_tap(k, carry):
        tap(k).start()
        return carry

    def take_tap(k, carry):
        tap(k).wait()
        return carry

    def gather_step(e, carry):
        arrive(e)

        @pl.when(e == 2)
        def _():
            prepare()

        @pl.when(e == 3)
        def _():
            lax.fori_loop(0, 27, load_tap, 0)
            loads[4].wait()
            loads[5].wait()
            wvo[...] = jnp.dot(wv[...], wo[...], preferred_element_type=F32).astype(BF16)

        low = jnp.where(e == 3, 1, e - 1)
        low = jnp.where(e == 2, 0, low)
        high = jnp.where(e == 2, 1, e)
        high = jnp.where(e == steps - 2, steps - 1, high)
        high = jnp.where(e == 1, low, high)
        low = jnp.where(e == steps - 1, high, low)
        lax.fori_loop(low, high, attend_step, 0)
        return carry

    lax.fori_loop(1, steps, gather_step, 0)
    attend(steps - 1, 0, 2)
    sib_copy(steps - 1).wait_recv()
    attend(steps - 1, 2, 2)

    def halo_up(which):
        return remote(
            act.at[which, 1], act.at[which, 3], edge_send.at[2 * which], edge_recv.at[2 * which], (t, above)
        )

    def halo_down(which):
        return remote(
            act.at[which, 2], act.at[which, 0], edge_send.at[2 * which + 1], edge_recv.at[2 * which + 1], (t, below)
        )

    def onward(row):
        return remote(
            act.at[0, 1 + row], act.at[1, 1 + row], edge_send.at[4 + row], edge_recv.at[4 + row], (t_next, i)
        )

    def send_halo(which, row):
        @pl.when(row == 0)
        def _():
            halo_up(which).start()

        @pl.when(row == 1)
        def _():
            halo_down(which).start()

    def finish(k, carry):
        row = k + core - 2 * k * core
        part = pl.ds(pl.multiple_of(row * cols, cols), cols)
        mixed = (acc[part, :] * (1.0 / total[part, 0:1]) * ab[0:1] + ab[1:2]).astype(BF16)
        change = jnp.dot(mixed, wvo[...], preferred_element_type=F32)
        mid_row = (slots[0, row].astype(F32) + change).astype(BF16)
        mid[part, :] = mid_row
        wide = mid_row.astype(F32)
        act[0, 1 + row] = (wide * (1.0 / (1.0 + jnp.exp(-wide)))).astype(BF16)

        @pl.when(has_next)
        def _():
            onward(row).start()

        send_halo(0, row)
        return carry

    lax.fori_loop(0, 2, finish, 0)

    loads[6].wait()
    skip = jnp.dot(mid[...], ws[...], preferred_element_type=F32)
    base[:, :outs] = skip
    base[:, outs:] = skip
    near[...] = jnp.zeros_like(near)
    far[...] = jnp.zeros_like(far)
    lax.fori_loop(0, 27, take_tap, 0)

    def visit(n):
        own = n < 4
        first = lax.rem(n, 2) == 0
        inner = n // 2
        mine = jnp.where(inner == 0, 1 + core, 2 - core)
        halo = jnp.where(first, 3 * core, 3 - 3 * core)
        source = jnp.where(own, mine, halo)
        same = jnp.where(inner == 0, core, 1 - core)
        target = jnp.where(own, jnp.where(first, same, 1 - same), jnp.where(first, core, 1 - core))
        return source, target, source - target

    def add_row(sums, which, n, start):
        source, target, dy = visit(n)
        row = act[which, source]
        part = pl.ds(pl.multiple_of(target * cols, cols), cols)
        for dx in range(3):
            sums[dx, part, :] += jnp.dot(row, wc[dx, dy, :, start:start + 2 * outs], preferred_element_type=F32)

    position = lax.rem(lax.broadcasted_iota(jnp.int32, (cells, 1), 0), cols)

    def shifted(z, dx):
        if dx == 0:
            return jnp.where(position == 0, 0.0, pltpu.roll(z, 1, 0))
        if dx == 2:
            return jnp.where(position == cols - 1, 0.0, pltpu.roll(z, cells - 1, 0))
        return z

    at_rim = jnp.where(core == 0, i == 0, i == tiles - 1)

    def near_step(n, carry):
        @pl.when(n == 4)
        def _():
            halo_up(0).wait_recv()
            halo_down(0).wait_recv()

        @pl.when(jnp.logical_not(jnp.logical_and(n == 4, at_rim)))
        def _():
            add_row(near, 0, n, outs)

        return carry

    lax.fori_loop(0, 6, near_step, 0)
    which = jnp.where(t == 0, 0, 1)

    def far_step(n, carry):
        @pl.when(jnp.logical_and(has_prev, lax.rem(n, 2) == 0))
        def _():
            row = jnp.where(n == 0, core, 1 - core)
            onward(row).wait_recv()
            send_halo(1, row)

        add_row(far, which, n, 0)

        @pl.when(n == 1)
        def _():
            for dx in range(3):
                z = shifted(near[dx], dx)
                base[:, :outs] += z[:, outs:]
                base[:, outs:] += z[:, :outs] + z[:, outs:]

        return carry

    lax.fori_loop(0, 4, far_step, 0)
    for dx in range(3):
        z = shifted(far[dx], dx)
        base[:, :outs] += z[:, :outs] + z[:, outs:]
        base[:, outs:] += z[:, :outs]

    place = lax.broadcasted_iota(jnp.int32, (cols, 1), 0)

    def last_step(n, carry):
        from_above = jnp.where(n == 4, core == 0, core == 1)

        @pl.when(jnp.logical_and(has_prev, from_above))
        def _():
            halo_down(1).wait_recv()

        @pl.when(jnp.logical_and(has_prev, jnp.logical_not(from_above)))
        def _():
            halo_up(1).wait_recv()

        source, target, dy = visit(n)
        row = act[which, source]
        row = jnp.where(jnp.logical_and(n == 4, at_rim), jnp.zeros_like(row), row)
        part = pl.ds(pl.multiple_of(target * cols, cols), cols)
        even = base[part, :outs]
        odd = base[part, outs:]
        for dx in range(3):
            z = jnp.dot(row, wc[dx, dy, :, :2 * outs], preferred_element_type=F32)
            if dx == 0:
                z = jnp.where(place == 0, 0.0, pltpu.roll(z, 1, 0))
            if dx == 2:
                z = jnp.where(place == cols - 1, 0.0, pltpu.roll(z, cols - 1, 0))
            even = even + (z[:, :outs] + z[:, outs:])
            odd = odd + z[:, :outs]
        out_ref[0, part, :] = even.astype(BF16)
        out_ref[1, part, :] = odd.astype(BF16)
        return carry

    lax.fori_loop(4, 6, last_step, 0)

    for h in range(2):
        for lane in range(2):
            first(h, lane).wait_send()
    own_to_sibling.wait_send()

    def drain(e, carry):
        for lane in range(2):
            @pl.when(e < steps - 2)
            def _():
                ring_copy(e, lane).wait_send()
        sib_copy(e).wait_send()
        return carry

    lax.fori_loop(1, steps, drain, 0)

    def drain_stat(k, carry):
        stat_copy(k).wait_send()
        return carry

    lax.fori_loop(1, tiles, drain_stat, 0)
    halo_up(0).wait_send()
    halo_down(0).wait_send()

    @pl.when(has_prev)
    def _():
        halo_up(1).wait_send()
        halo_down(1).wait_send()

    @pl.when(has_next)
    def _():
        for row in range(2):
            onward(row).wait_send()


def per_device(
    spans, tiles, features, norm_gain, query_weight, key_weight, value_weight, out_weight, conv_weight, skip_weight
):
    frames, rows, cols, channels = features.shape
    outs = conv_weight.shape[-1]
    cells = rows * cols
    steps = tiles // 2
    hbm = pl.BlockSpec(memory_space=pltpu.HBM)
    dma = pltpu.SemaphoreType.DMA
    operands = (
        features.reshape(rows, cols, channels), norm_gain.reshape(1, channels),
        query_weight, key_weight, value_weight, out_weight, conv_weight, skip_weight,
    )
    operands = [pltpu.with_memory_space_constraint(operand, pltpu.HBM) for operand in operands]
    out = pl.pallas_call(
        functools.partial(kernel, spans, tiles),
        out_shape=jax.ShapeDtypeStruct((2, cells, outs), BF16),
        in_specs=[hbm] * 8,
        out_specs=pl.BlockSpec(memory_space=pltpu.VMEM),
        scratch_shapes=[
            pltpu.VMEM((steps, 4, cols, channels), BF16),
            pltpu.VMEM((cells, channels), BF16),
            pltpu.VMEM((cells, channels), F32),
            pltpu.VMEM((cells, 128), F32),
            pltpu.VMEM((cells, 128), F32),
            pltpu.VMEM((tiles, 1, 128), F32),
            pltpu.VMEM((8, channels), F32),
            pltpu.VMEM((1, channels), F32),
            pltpu.VMEM((channels, channels), BF16),
            pltpu.VMEM((channels, channels), BF16),
            pltpu.VMEM((channels, channels), BF16),
            pltpu.VMEM((channels, channels), BF16),
            pltpu.VMEM((channels, channels), BF16),
            pltpu.VMEM((channels, outs), BF16),
            pltpu.VMEM((2, 4, cols, channels), BF16),
            pltpu.VMEM((cells, channels), BF16),
            pltpu.VMEM((3, cells, 2 * outs), F32),
            pltpu.VMEM((3, cells, 2 * outs), F32),
            pltpu.VMEM((cells, 2 * outs), F32),
            pltpu.VMEM((3, 3, channels, 3 * outs), BF16),
            dma((steps, 2)), dma((steps, 2)), dma((steps,)), dma((steps,)), dma((tiles,)), dma((tiles,)), dma((7,)),
            dma((6,)), dma((6,)), dma((27,)),
        ],
        compiler_params=pltpu.CompilerParams(
            collective_id=0, has_side_effects=True, vmem_limit_bytes=50 * 1024 * 1024
        ),
        name="mid_block_decode",
    )(*operands)
    return out.reshape(2 * frames, rows, cols, outs)


def solution(mesh):
    spans, tiles = mesh.shape["tm"], mesh.shape["tile"]
    in_specs = (P("tm", "tile", None, None), P(), P(), P(), P(), P(), P(), P())
    return jax.shard_map(
        functools.partial(per_device, spans, tiles), mesh=mesh, in_specs=in_specs,
        out_specs=P("tm", "tile", None, None), check_vma=False,
    )
```

```python
import functools
import math

import jax
import jax.numpy as jnp
from jax import lax
from jax.experimental import pallas as pl
from jax.experimental.pallas import tpu as pltpu
from jax.sharding import PartitionSpec as P

GROUPS = 32
EPS = 1e-06
MESH = pl.DeviceIdType.MESH
F32 = jnp.float32
BF16 = jnp.bfloat16


def group_sum(v, width):
    lanes = v.shape[-1]
    lane = lax.broadcasted_iota(jnp.int32, v.shape, 1)
    step = 1
    while step < width:
        above = pltpu.roll(v, lanes - step, 1)
        below = pltpu.roll(v, step, 1)
        v = v + jnp.where((lane & step) == 0, above, below)
        step *= 2
    return v


def remote(src, dst, send, recv, where):
    return pltpu.make_async_remote_copy(
        src_ref=src, dst_ref=dst, send_sem=send, recv_sem=recv, device_id=where, device_id_type=MESH
    )


def kernel(
    spans, tiles, x_hbm, gain_hbm, wq_hbm, wk_hbm, wv_hbm, wo_hbm, wc_hbm, ws_hbm, out_ref,
    slots, q2, acc, peak, total, stats, ab, gain, wq, wk, wv, wo, wvo, ws,
    act, mid, near, far, base, wc,
    ring_send, ring_recv, sib_send, sib_recv, st_send, st_recv, load_sem, edge_send, edge_recv, conv_sem,
):
    rows, cols, channels = x_hbm.shape
    outs = ws.shape[1]
    cells = rows * cols
    width = channels // GROUPS
    blocks = channels // 128
    steps = tiles // 2

    t = lax.axis_index("tm")
    i = lax.axis_index("tile")
    y = i // 2
    core = i - 2 * y
    right = lax.rem(i + 2, tiles)
    left = lax.rem(i + tiles - 2, tiles)
    sibling = 2 * y + 1 - core
    above = lax.rem(i + tiles - 1, tiles)
    below = lax.rem(i + 1, tiles)
    t_next = lax.rem(t + 1, spans)
    t_prev = lax.rem(t + spans - 1, spans)
    has_next = t < spans - 1
    has_prev = t > 0

    loads = [
        pltpu.make_async_copy(x_hbm, slots.at[0, pl.ds(0, 2)], load_sem.at[0]),
        pltpu.make_async_copy(wq_hbm, wq, load_sem.at[1]),
        pltpu.make_async_copy(wk_hbm, wk, load_sem.at[2]),
        pltpu.make_async_copy(gain_hbm, gain, load_sem.at[3]),
        pltpu.make_async_copy(wv_hbm, wv, load_sem.at[4]),
        pltpu.make_async_copy(wo_hbm, wo, load_sem.at[5]),
        pltpu.make_async_copy(ws_hbm, ws, load_sem.at[6]),
    ]
    loads[0].start()

    barrier = pltpu.get_barrier_semaphore()

    edge_peer = jnp.where(core == 0, above, below)
    for peer in (right, left, sibling, edge_peer):
        pl.semaphore_signal(barrier, inc=1, device_id=(t, peer), device_id_type=MESH)

    @pl.when(has_prev)
    def _():
        pl.semaphore_signal(barrier, inc=1, device_id=(t_prev, i), device_id_type=MESH)

    loads[0].wait()
    pl.semaphore_wait(barrier, 4 + jnp.where(has_next, 1, 0))

    def first(h, lane):
        row = h if lane == 0 else 1 - h
        return remote(
            slots.at[0, row], slots.at[1 + h, lane], ring_send.at[1 + h, lane], ring_recv.at[1 + h, lane],
            (t, right if lane == 0 else left),
        )

    for lane in range(2):
        first(0, lane).start()
    own_to_sibling = remote(
        slots.at[0, pl.ds(0, 2)], slots.at[0, pl.ds(2, 2)], sib_send.at[0], sib_recv.at[0], (t, sibling)
    )
    own_to_sibling.start()

    own = slots[0, 0:2].reshape(cells, channels).astype(F32)
    sums = jnp.sum(own, axis=0, keepdims=True)
    squares = jnp.sum(own * own, axis=0, keepdims=True)
    sums = group_sum(jnp.broadcast_to(sums, (8, channels)), width)
    squares = group_sum(jnp.broadcast_to(squares, (8, channels)), width)
    lane_of = lax.broadcasted_iota(jnp.int32, (8, 128), 1) & (width - 1)
    packed = jnp.zeros((8, 128), F32)
    for k in range(2 * blocks):
        source = sums if k < blocks else squares
        b = k % blocks
        packed = jnp.where(lane_of == k, source[:, b * 128:(b + 1) * 128], packed)
    stats[0] = packed[0:1]

    half = steps // 2

    def sums_right(d):
        return remote(
            stats.at[d - 1], stats.at[d], st_send.at[d], st_recv.at[d], (t, right)
        )

    def sums_left(d):
        source = jnp.where(d == 1, 0, half + d - 1)
        return remote(
            stats.at[source], stats.at[half + d], st_send.at[half + d], st_recv.at[half + d], (t, left)
        )

    sums_across = remote(stats.at[steps], stats.at[steps + 1], st_send.at[steps], st_recv.at[steps], (t, sibling))

    def relay(d):
        sums_right(d).wait_recv()
        sums_right(d + 1).start()
        sums_left(d).wait_recv()

        @pl.when(d < half - 1)
        def _():
            sums_left(d + 1).start()

    sums_right(1).start()
    sums_left(1).start()
    for lane in range(2):
        first(1, lane).start()
    for copy in loads[1:]:
        copy.start()

    def ring_copy(e, lane):
        return remote(
            slots.at[e, lane], slots.at[e + 2, lane], ring_send.at[e + 2, lane], ring_recv.at[e + 2, lane],
            (t, right if lane == 0 else left),
        )

    def ring_arrival(e, lane):
        return remote(
            slots.at[e, lane], slots.at[e, lane], ring_send.at[e, lane], ring_recv.at[e, lane],
            (t, right if lane == 0 else left),
        )

    def sib_copy(e):
        return remote(
            slots.at[e, pl.ds(0, 2)], slots.at[e, pl.ds(2, 2)], sib_send.at[e], sib_recv.at[e], (t, sibling)
        )

    def prepare():
        sums_right(half).wait_recv()
        whole = stats[0]
        for k in range(1, steps):
            whole = whole + stats[k]
        stats[steps] = whole
        sums_across.start()
        sums_across.wait_recv()
        whole = whole + stats[steps + 1]
        whole = jnp.broadcast_to(whole, (8, 128))
        spread = [group_sum(jnp.where(lane_of == k, whole, 0.0), width) for k in range(2 * blocks)]
        population = float(tiles * cells * width)
        mean = jnp.concatenate(spread[:blocks], axis=1)[0:1] / population
        var = jnp.concatenate(spread[blocks:], axis=1)[0:1] / population - mean * mean
        rstd = lax.rsqrt(var + EPS)
        loads[3].wait()
        scaled = rstd * gain[...]
        ab[0:1] = scaled
        ab[1:2] = -mean * scaled
        block = slots[0, 0:2].reshape(cells, channels).astype(F32)
        normed = (((block - mean) * rstd) * gain[...]).astype(BF16)
        loads[1].wait()
        queries = jnp.dot(normed, wq[...], preferred_element_type=F32).astype(BF16)
        loads[2].wait()
        inner = lax.dot_general(queries, wk[...], (((1,), (1,)), ((), ())), preferred_element_type=F32)
        scale = channels ** (-0.5) * math.log2(math.e)
        q2[...] = (inner * (scaled * scale)).astype(BF16)
        acc[...] = jnp.zeros_like(acc)
        total[...] = jnp.zeros_like(total)
        peak[...] = jnp.full_like(peak, -jnp.inf)

    def attend(e, begin, count):
        keys = slots[e, begin:begin + count].reshape(count * cols, channels)
        scores = lax.dot_general(q2[...], keys, (((1,), (1,)), ((), ())), preferred_element_type=F32)
        before = peak[:, 0:1]
        now = jnp.maximum(before, jnp.max(scores, axis=1, keepdims=True))
        fade = jnp.exp2(before - now)
        weights = jnp.exp2(scores - now).astype(BF16)
        peak[...] = jnp.broadcast_to(now, peak.shape)
        total[...] = total[...] * fade + jnp.sum(weights.astype(F32), axis=1, keepdims=True)
        acc[...] = acc[...] * fade + jnp.dot(weights, keys, preferred_element_type=F32)

    def arrive(e):
        for lane in range(2):
            ring_arrival(e, lane).wait_recv()

            @pl.when(e < steps - 2)
            def _():
                ring_copy(e, lane).start()

        sib_copy(e).start()

    def attend_step(e, carry):
        sib_copy(e).wait_recv()
        attend(e, 0, 4)
        return carry

    def tap(k):
        dt = k // 9
        dy = (k - 9 * dt) // 3
        dx = k - 9 * dt - 3 * dy
        column = pl.multiple_of(dt * outs, outs)
        return pltpu.make_async_copy(wc_hbm.at[dt, dy, dx], wc.at[dx, dy, :, pl.ds(column, outs)], conv_sem.at[k])

    def load_tap(k, carry):
        tap(k).start()
        return carry

    def take_tap(k, carry):
        tap(k).wait()
        return carry

    def tap(k):
        dt = k // 9
        dy = (k - 9 * dt) // 3
        dx = k - 9 * dt - 3 * dy
        column = pl.multiple_of(dt * outs, outs)
        return pltpu.make_async_copy(wc_hbm.at[dt, dy, dx], wc.at[dx, dy, :, pl.ds(column, outs)], conv_sem.at[k])

    def load_tap(k, carry):
        tap(k).start()
        return carry

    def take_tap(k, carry):
        tap(k).wait()
        return carry

    def gather_step(e, carry):
        @pl.when(e < half)
        def _():
            relay(e)

        arrive(e)

        @pl.when(e == 2)
        def _():
            lax.fori_loop(0, 27, load_tap, 0)
            loads[4].wait()
            loads[5].wait()
            wvo[...] = jnp.dot(wv[...], wo[...], preferred_element_type=F32).astype(BF16)

        @pl.when(e == half)
        def _():
            prepare()

        low = jnp.where(e <= half, 0, 3 * (e - half - 1))
        high = jnp.where(e <= half, 0, low + 3)
        high = jnp.where(e == steps - 1, low, high)
        lax.fori_loop(low, high, attend_step, 0)
        return carry

    lax.fori_loop(1, steps, gather_step, 0)
    attend_step(steps - 2, 0)
    attend(steps - 1, 0, 2)
    sib_copy(steps - 1).wait_recv()
    attend(steps - 1, 2, 2)

    def halo_up(which):
        return remote(
            act.at[which, 1], act.at[which, 3], edge_send.at[2 * which], edge_recv.at[2 * which], (t, above)
        )

    def halo_down(which):
        return remote(
            act.at[which, 2], act.at[which, 0], edge_send.at[2 * which + 1], edge_recv.at[2 * which + 1], (t, below)
        )

    def onward(row):
        return remote(
            act.at[0, 1 + row], act.at[1, 1 + row], edge_send.at[4 + row], edge_recv.at[4 + row], (t_next, i)
        )

    across = remote(act.at[0, 0], act.at[1, 0], edge_send.at[6], edge_recv.at[6], (t_next, i))
    back = remote(act.at[1, 0], act.at[1, 2], edge_send.at[7], edge_recv.at[7], (t, above))

    def send_halo(which, row):
        @pl.when(row == 0)
        def _():
            halo_up(which).start()

        @pl.when(row == 1)
        def _():
            halo_down(which).start()

    def finish(k, carry):
        row = k + core - 2 * k * core
        part = pl.ds(pl.multiple_of(row * cols, cols), cols)
        mixed = (acc[part, :] * (1.0 / total[part, 0:1]) * ab[0:1] + ab[1:2]).astype(BF16)
        change = jnp.dot(mixed, wvo[...], preferred_element_type=F32)
        mid_row = (slots[0, row].astype(F32) + change).astype(BF16)
        mid[part, :] = mid_row
        wide = mid_row.astype(F32)
        act[0, 1 + row] = (wide * (1.0 / (1.0 + jnp.exp(-wide)))).astype(BF16)

        @pl.when(jnp.logical_and(has_next, k == 0))
        def _():
            onward(row).start()

        send_halo(0, row)
        return carry

    lax.fori_loop(0, 2, finish, 0)

    @pl.when(core == 1)
    def _():
        halo_down(0).wait_recv()

        @pl.when(has_next)
        def _():
            across.start()
            onward(0).start()


    loads[6].wait()
    skip = jnp.dot(mid[...], ws[...], preferred_element_type=F32)
    base[:, :outs] = skip
    base[:, outs:] = skip
    near[...] = jnp.zeros_like(near)
    far[...] = jnp.zeros_like(far)
    lax.fori_loop(0, 27, take_tap, 0)

    def visit(n):
        own = n < 4
        first = lax.rem(n, 2) == 0
        inner = n // 2
        mine = jnp.where(inner == 0, 1 + core, 2 - core)
        halo = jnp.where(first, 3 * core, 3 - 3 * core)
        source = jnp.where(own, mine, halo)
        same = jnp.where(inner == 0, core, 1 - core)
        target = jnp.where(own, jnp.where(first, same, 1 - same), jnp.where(first, core, 1 - core))
        return source, target, source - target

    def add_row(sums, which, n, start):
        source, target, dy = visit(n)
        row = act[which, source]
        part = pl.ds(pl.multiple_of(target * cols, cols), cols)
        for dx in range(3):
            sums[dx, part, :] += jnp.dot(row, wc[dx, dy, :, start:start + 2 * outs], preferred_element_type=F32)

    position = lax.rem(lax.broadcasted_iota(jnp.int32, (cells, 1), 0), cols)

    def shifted(z, dx):
        if dx == 0:
            return jnp.where(position == 0, 0.0, pltpu.roll(z, 1, 0))
        if dx == 2:
            return jnp.where(position == cols - 1, 0.0, pltpu.roll(z, cells - 1, 0))
        return z

    at_rim = jnp.where(core == 0, i == 0, i == tiles - 1)

    def near_step(n, carry):
        @pl.when(n == 4)
        def _():
            halo_up(0).wait_recv()

            @pl.when(core == 0)
            def _():
                halo_down(0).wait_recv()


        @pl.when(jnp.logical_not(jnp.logical_and(n == 4, at_rim)))
        def _():
            add_row(near, 0, n, outs)

        return carry

    lax.fori_loop(0, 6, near_step, 0)
    which = jnp.where(t == 0, 0, 1)

    def far_step(n, carry):
        @pl.when(jnp.logical_and(has_prev, n == 0))
        def _():
            onward(core).wait_recv()
            send_halo(1, core)

        @pl.when(jnp.logical_and(has_prev, n == 2))
        def _():
            @pl.when(core == 0)
            def _():
                back.wait_recv()

            @pl.when(core == 1)
            def _():
                across.wait_recv()
                back.start()
                onward(0).wait_recv()
                halo_up(1).start()

        add_row(far, which, n, 0)

        @pl.when(n == 1)
        def _():
            for dx in range(3):
                z = shifted(near[dx], dx)
                base[:, :outs] += z[:, outs:]
                base[:, outs:] += z[:, :outs] + z[:, outs:]

        return carry

    lax.fori_loop(0, 4, far_step, 0)
    for dx in range(3):
        z = shifted(far[dx], dx)
        base[:, :outs] += z[:, :outs] + z[:, outs:]
        base[:, outs:] += z[:, :outs]

    place = lax.broadcasted_iota(jnp.int32, (cols, 1), 0)

    def last_step(k, carry):
        n = jnp.where(core == 0, k, 9 - k)

        @pl.when(jnp.logical_and(has_prev, jnp.logical_and(core == 0, k == 4)))
        def _():
            halo_down(1).wait_recv()

        @pl.when(jnp.logical_and(has_prev, k == 5))
        def _():
            halo_up(1).wait_recv()

        source, target, dy = visit(n)
        row = act[which, source]
        row = jnp.where(jnp.logical_and(n == 4, at_rim), jnp.zeros_like(row), row)
        part = pl.ds(pl.multiple_of(target * cols, cols), cols)
        even = base[part, :outs]
        odd = base[part, outs:]
        for dx in range(3):
            z = jnp.dot(row, wc[dx, dy, :, :2 * outs], preferred_element_type=F32)
            if dx == 0:
                z = jnp.where(place == 0, 0.0, pltpu.roll(z, 1, 0))
            if dx == 2:
                z = jnp.where(place == cols - 1, 0.0, pltpu.roll(z, cols - 1, 0))
            even = even + (z[:, :outs] + z[:, outs:])
            odd = odd + z[:, :outs]
        out_ref[0, part, :] = even.astype(BF16)
        out_ref[1, part, :] = odd.astype(BF16)
        return carry

    lax.fori_loop(4, 6, last_step, 0)

    for h in range(2):
        for lane in range(2):
            first(h, lane).wait_send()
    own_to_sibling.wait_send()

    def drain(e, carry):
        for lane in range(2):
            @pl.when(e < steps - 2)
            def _():
                ring_copy(e, lane).wait_send()
        sib_copy(e).wait_send()
        return carry

    lax.fori_loop(1, steps, drain, 0)

    for d in range(1, half + 1):
        sums_right(d).wait_send()
    for d in range(1, half):
        sums_left(d).wait_send()
    sums_across.wait_send()
    halo_up(0).wait_send()
    halo_down(0).wait_send()

    @pl.when(has_prev)
    def _():
        halo_up(1).wait_send()

        @pl.when(core == 1)
        def _():
            halo_down(1).wait_send()
            back.wait_send()

    @pl.when(has_next)
    def _():
        onward(0).wait_send()

        @pl.when(core == 1)
        def _():
            onward(1).wait_send()
            across.wait_send()


def per_device(
    spans, tiles, features, norm_gain, query_weight, key_weight, value_weight, out_weight, conv_weight, skip_weight
):
    frames, rows, cols, channels = features.shape
    outs = conv_weight.shape[-1]
    cells = rows * cols
    steps = tiles // 2
    hbm = pl.BlockSpec(memory_space=pltpu.HBM)
    dma = pltpu.SemaphoreType.DMA
    operands = (
        features.reshape(rows, cols, channels), norm_gain.reshape(1, channels),
        query_weight, key_weight, value_weight, out_weight, conv_weight, skip_weight,
    )
    operands = [pltpu.with_memory_space_constraint(operand, pltpu.HBM) for operand in operands]
    out = pl.pallas_call(
        functools.partial(kernel, spans, tiles),
        out_shape=jax.ShapeDtypeStruct((2, cells, outs), BF16),
        in_specs=[hbm] * 8,
        out_specs=pl.BlockSpec(memory_space=pltpu.VMEM),
        scratch_shapes=[
            pltpu.VMEM((steps, 4, cols, channels), BF16),
            pltpu.VMEM((cells, channels), BF16),
            pltpu.VMEM((cells, channels), F32),
            pltpu.VMEM((cells, 128), F32),
            pltpu.VMEM((cells, 128), F32),
            pltpu.VMEM((steps + 2, 1, 128), F32),
            pltpu.VMEM((8, channels), F32),
            pltpu.VMEM((1, channels), F32),
            pltpu.VMEM((channels, channels), BF16),
            pltpu.VMEM((channels, channels), BF16),
            pltpu.VMEM((channels, channels), BF16),
            pltpu.VMEM((channels, channels), BF16),
            pltpu.VMEM((channels, channels), BF16),
            pltpu.VMEM((channels, outs), BF16),
            pltpu.VMEM((2, 4, cols, channels), BF16),
            pltpu.VMEM((cells, channels), BF16),
            pltpu.VMEM((3, cells, 2 * outs), F32),
            pltpu.VMEM((3, cells, 2 * outs), F32),
            pltpu.VMEM((cells, 2 * outs), F32),
            pltpu.VMEM((3, 3, channels, 3 * outs), BF16),
            dma((steps, 2)), dma((steps, 2)), dma((steps,)), dma((steps,)), dma((steps + 1,)), dma((steps + 1,)), dma((7,)),
            dma((8,)), dma((8,)), dma((27,)),
        ],
        compiler_params=pltpu.CompilerParams(
            collective_id=0, has_side_effects=True, vmem_limit_bytes=50 * 1024 * 1024
        ),
        name="mid_block_decode",
    )(*operands)
    return out.reshape(2 * frames, rows, cols, outs)


def solution(mesh):
    spans, tiles = mesh.shape["tm"], mesh.shape["tile"]
    in_specs = (P("tm", "tile", None, None), P(), P(), P(), P(), P(), P(), P())
    return jax.shard_map(
        functools.partial(per_device, spans, tiles), mesh=mesh, in_specs=in_specs,
        out_specs=P("tm", "tile", None, None), check_vma=False,
    )
```

```python
import functools
import math

import jax
import jax.numpy as jnp
from jax import lax
from jax.experimental import pallas as pl
from jax.experimental.pallas import tpu as pltpu
from jax.sharding import PartitionSpec as P

GROUPS = 32
EPS = 1e-06
MESH = pl.DeviceIdType.MESH
F32 = jnp.float32
BF16 = jnp.bfloat16


def group_sum(v, width):
    lanes = v.shape[-1]
    lane = lax.broadcasted_iota(jnp.int32, v.shape, 1)
    step = 1
    while step < width:
        above = pltpu.roll(v, lanes - step, 1)
        below = pltpu.roll(v, step, 1)
        v = v + jnp.where((lane & step) == 0, above, below)
        step *= 2
    return v


def remote(src, dst, send, recv, where):
    return pltpu.make_async_remote_copy(
        src_ref=src, dst_ref=dst, send_sem=send, recv_sem=recv, device_id=where, device_id_type=MESH
    )


def kernel(
    spans, tiles, x_hbm, gain_hbm, wq_hbm, wk_hbm, wv_hbm, wo_hbm, wc_hbm, ws_hbm, out_ref,
    slots, q2, acc, peak, total, stats, ab, gain, wq, wk, wv, wo, wvo, ws,
    act, mid, near, far, base, wc,
    ring_send, ring_recv, sib_send, sib_recv, st_send, st_recv, load_sem, edge_send, edge_recv, conv_sem,
):
    rows, cols, channels = x_hbm.shape
    outs = ws.shape[1]
    cells = rows * cols
    width = channels // GROUPS
    blocks = channels // 128
    steps = tiles // 2

    t = lax.axis_index("tm")
    i = lax.axis_index("tile")
    y = i // 2
    core = i - 2 * y
    right = lax.rem(i + 2, tiles)
    left = lax.rem(i + tiles - 2, tiles)
    sibling = 2 * y + 1 - core
    above = lax.rem(i + tiles - 1, tiles)
    below = lax.rem(i + 1, tiles)
    t_next = lax.rem(t + 1, spans)
    t_prev = lax.rem(t + spans - 1, spans)
    has_next = t < spans - 1
    has_prev = t > 0

    loads = [
        pltpu.make_async_copy(x_hbm, slots.at[0, pl.ds(0, 2)], load_sem.at[0]),
        pltpu.make_async_copy(wq_hbm, wq, load_sem.at[1]),
        pltpu.make_async_copy(wk_hbm, wk, load_sem.at[2]),
        pltpu.make_async_copy(gain_hbm, gain, load_sem.at[3]),
        pltpu.make_async_copy(wv_hbm, wv, load_sem.at[4]),
        pltpu.make_async_copy(wo_hbm, wo, load_sem.at[5]),
        pltpu.make_async_copy(ws_hbm, ws, load_sem.at[6]),
    ]
    loads[0].start()

    barrier = pltpu.get_barrier_semaphore()

    edge_peer = jnp.where(core == 0, above, below)
    for peer in (right, left, sibling, edge_peer):
        pl.semaphore_signal(barrier, inc=1, device_id=(t, peer), device_id_type=MESH)

    @pl.when(has_prev)
    def _():
        pl.semaphore_signal(barrier, inc=1, device_id=(t_prev, i), device_id_type=MESH)

    loads[0].wait()
    pl.semaphore_wait(barrier, 4 + jnp.where(has_next, 1, 0))

    def first(h, lane):
        row = h if lane == 0 else 1 - h
        return remote(
            slots.at[0, row], slots.at[1 + h, lane], ring_send.at[1 + h, lane], ring_recv.at[1 + h, lane],
            (t, right if lane == 0 else left),
        )

    for lane in range(2):
        first(0, lane).start()
    own_to_sibling = remote(
        slots.at[0, pl.ds(0, 2)], slots.at[0, pl.ds(2, 2)], sib_send.at[0], sib_recv.at[0], (t, sibling)
    )
    own_to_sibling.start()

    own = slots[0, 0:2].reshape(cells, channels).astype(F32)
    sums = jnp.sum(own, axis=0, keepdims=True)
    squares = jnp.sum(own * own, axis=0, keepdims=True)
    sums = group_sum(jnp.broadcast_to(sums, (8, channels)), width)
    squares = group_sum(jnp.broadcast_to(squares, (8, channels)), width)
    lane_of = lax.broadcasted_iota(jnp.int32, (8, 128), 1) & (width - 1)
    packed = jnp.zeros((8, 128), F32)
    for k in range(2 * blocks):
        source = sums if k < blocks else squares
        b = k % blocks
        packed = jnp.where(lane_of == k, source[:, b * 128:(b + 1) * 128], packed)
    stats[tiles // 2] = packed[0:1]

    half = steps // 2

    def sums_right(d):
        return remote(
            stats.at[d - 1], stats.at[d], st_send.at[d], st_recv.at[d], (t, right)
        )

    def sums_left(d):
        source = jnp.where(d == 1, 0, half + d - 1)
        return remote(
            stats.at[source], stats.at[half + d], st_send.at[half + d], st_recv.at[half + d], (t, left)
        )

    sums_across = remote(stats.at[steps], stats.at[steps + 1], st_send.at[steps], st_recv.at[steps], (t, sibling))

    def relay(d):
        sums_right(d).wait_recv()
        sums_right(d + 1).start()
        sums_left(d).wait_recv()

        @pl.when(d < half - 1)
        def _():
            sums_left(d + 1).start()

    sums_across.start()
    sums_across.wait_recv()
    stats[0] = stats[steps] + stats[steps + 1]
    sums_right(1).start()
    sums_left(1).start()
    for lane in range(2):
        first(1, lane).start()
    for copy in loads[1:]:
        copy.start()

    def ring_copy(e, lane):
        return remote(
            slots.at[e, lane], slots.at[e + 2, lane], ring_send.at[e + 2, lane], ring_recv.at[e + 2, lane],
            (t, right if lane == 0 else left),
        )

    def ring_arrival(e, lane):
        return remote(
            slots.at[e, lane], slots.at[e, lane], ring_send.at[e, lane], ring_recv.at[e, lane],
            (t, right if lane == 0 else left),
        )

    def sib_copy(e):
        return remote(
            slots.at[e, pl.ds(0, 2)], slots.at[e, pl.ds(2, 2)], sib_send.at[e], sib_recv.at[e], (t, sibling)
        )

    def prepare():
        sums_right(half).wait_recv()
        whole = stats[0]
        for k in range(1, steps):
            whole = whole + stats[k]
        whole = jnp.broadcast_to(whole, (8, 128))
        spread = [group_sum(jnp.where(lane_of == k, whole, 0.0), width) for k in range(2 * blocks)]
        population = float(tiles * cells * width)
        mean = jnp.concatenate(spread[:blocks], axis=1)[0:1] / population
        var = jnp.concatenate(spread[blocks:], axis=1)[0:1] / population - mean * mean
        rstd = lax.rsqrt(var + EPS)
        loads[3].wait()
        scaled = rstd * gain[...]
        ab[0:1] = scaled
        ab[1:2] = -mean * scaled
        block = slots[0, 0:2].reshape(cells, channels).astype(F32)
        normed = (((block - mean) * rstd) * gain[...]).astype(BF16)
        loads[1].wait()
        queries = jnp.dot(normed, wq[...], preferred_element_type=F32).astype(BF16)
        loads[2].wait()
        inner = lax.dot_general(queries, wk[...], (((1,), (1,)), ((), ())), preferred_element_type=F32)
        scale = channels ** (-0.5) * math.log2(math.e)
        q2[...] = (inner * (scaled * scale)).astype(BF16)
        acc[...] = jnp.zeros_like(acc)
        total[...] = jnp.zeros_like(total)
        peak[...] = jnp.full_like(peak, -jnp.inf)

    everything = pl.ds(0, cells)

    def attend(e, begin, count, part=everything):
        keys = slots[e, begin:begin + count].reshape(count * cols, channels)
        scores = lax.dot_general(q2[part, :], keys, (((1,), (1,)), ((), ())), preferred_element_type=F32)
        before = peak[part, 0:1]
        now = jnp.maximum(before, jnp.max(scores, axis=1, keepdims=True))
        fade = jnp.exp2(before - now)
        weights = jnp.exp2(scores - now).astype(BF16)
        peak[part, :] = jnp.broadcast_to(now, (now.shape[0], 128))
        total[part, :] = total[part, :] * fade + jnp.sum(weights.astype(F32), axis=1, keepdims=True)
        acc[part, :] = acc[part, :] * fade + jnp.dot(weights, keys, preferred_element_type=F32)

    def arrive(e):
        for lane in range(2):
            ring_arrival(e, lane).wait_recv()

            @pl.when(e < steps - 2)
            def _():
                ring_copy(e, lane).start()

        sib_copy(e).start()

    def attend_step(e, carry):
        sib_copy(e).wait_recv()
        attend(e, 0, 4)
        return carry

    def tap(k):
        dt = k // 9
        dy = (k - 9 * dt) // 3
        dx = k - 9 * dt - 3 * dy
        column = pl.multiple_of(dt * outs, outs)
        return pltpu.make_async_copy(wc_hbm.at[dt, dy, dx], wc.at[dx, dy, :, pl.ds(column, outs)], conv_sem.at[k])

    def load_tap(k, carry):
        tap(k).start()
        return carry

    def take_tap(k, carry):
        tap(k).wait()
        return carry

    def tap(k):
        dt = k // 9
        dy = (k - 9 * dt) // 3
        dx = k - 9 * dt - 3 * dy
        column = pl.multiple_of(dt * outs, outs)
        return pltpu.make_async_copy(wc_hbm.at[dt, dy, dx], wc.at[dx, dy, :, pl.ds(column, outs)], conv_sem.at[k])

    def load_tap(k, carry):
        tap(k).start()
        return carry

    def take_tap(k, carry):
        tap(k).wait()
        return carry

    def gather_step(e, carry):
        @pl.when(e < half)
        def _():
            relay(e)

        arrive(e)

        @pl.when(e == 2)
        def _():
            lax.fori_loop(0, 27, load_tap, 0)
            loads[4].wait()
            loads[5].wait()
            wvo[...] = jnp.dot(wv[...], wo[...], preferred_element_type=F32).astype(BF16)

        @pl.when(e == half)
        def _():
            prepare()

        low = jnp.where(e <= half, 0, jnp.where(e == half + 1, 1, half))
        high = jnp.where(e <= half, 1, jnp.where(e == half + 1, half, steps - 2))
        high = jnp.where(e < half, 0, high)
        high = jnp.where(e == steps - 1, low, high)
        lax.fori_loop(low, high, attend_step, 0)
        return carry

    lax.fori_loop(1, steps, gather_step, 0)
    attend_step(steps - 2, 0)
    attend(steps - 1, 0, 2)
    sib_copy(steps - 1).wait_recv()

    def halo_up(which):
        return remote(
            act.at[which, 1], act.at[which, 3], edge_send.at[2 * which], edge_recv.at[2 * which], (t, above)
        )

    def halo_down(which):
        return remote(
            act.at[which, 2], act.at[which, 0], edge_send.at[2 * which + 1], edge_recv.at[2 * which + 1], (t, below)
        )

    def onward(row):
        return remote(
            act.at[0, 1 + row], act.at[1, 1 + row], edge_send.at[4 + row], edge_recv.at[4 + row], (t_next, i)
        )

    across = remote(act.at[0, 0], act.at[1, 0], edge_send.at[6], edge_recv.at[6], (t_next, i))
    back = remote(act.at[1, 0], act.at[1, 2], edge_send.at[7], edge_recv.at[7], (t, above))

    def send_halo(which, row):
        @pl.when(row == 0)
        def _():
            halo_up(which).start()

        @pl.when(row == 1)
        def _():
            halo_down(which).start()

    def finish(k, carry):
        row = k + core - 2 * k * core
        part = pl.ds(pl.multiple_of(row * cols, cols), cols)
        attend(steps - 1, 2, 2, part)
        mixed = (acc[part, :] * (1.0 / total[part, 0:1]) * ab[0:1] + ab[1:2]).astype(BF16)
        change = jnp.dot(mixed, wvo[...], preferred_element_type=F32)
        mid_row = (slots[0, row].astype(F32) + change).astype(BF16)
        mid[part, :] = mid_row
        wide = mid_row.astype(F32)
        act[0, 1 + row] = (wide * (1.0 / (1.0 + jnp.exp(-wide)))).astype(BF16)

        @pl.when(jnp.logical_and(has_next, k == 0))
        def _():
            onward(row).start()

        send_halo(0, row)
        return carry

    lax.fori_loop(0, 2, finish, 0)

    @pl.when(core == 1)
    def _():
        halo_down(0).wait_recv()

        @pl.when(has_next)
        def _():
            across.start()
            onward(0).start()


    loads[6].wait()
    skip = jnp.dot(mid[...], ws[...], preferred_element_type=F32)
    base[:, :outs] = skip
    base[:, outs:] = skip
    near[...] = jnp.zeros_like(near)
    far[...] = jnp.zeros_like(far)
    lax.fori_loop(0, 27, take_tap, 0)

    def visit(n):
        own = n < 4
        first = lax.rem(n, 2) == 0
        inner = n // 2
        mine = jnp.where(inner == 0, 1 + core, 2 - core)
        halo = jnp.where(first, 3 * core, 3 - 3 * core)
        source = jnp.where(own, mine, halo)
        same = jnp.where(inner == 0, core, 1 - core)
        target = jnp.where(own, jnp.where(first, same, 1 - same), jnp.where(first, core, 1 - core))
        return source, target, source - target

    def add_row(sums, which, n, start):
        source, target, dy = visit(n)
        row = act[which, source]
        part = pl.ds(pl.multiple_of(target * cols, cols), cols)
        for dx in range(3):
            sums[dx, part, :] += jnp.dot(row, wc[dx, dy, :, start:start + 2 * outs], preferred_element_type=F32)

    position = lax.rem(lax.broadcasted_iota(jnp.int32, (cells, 1), 0), cols)

    def shifted(z, dx):
        if dx == 0:
            return jnp.where(position == 0, 0.0, pltpu.roll(z, 1, 0))
        if dx == 2:
            return jnp.where(position == cols - 1, 0.0, pltpu.roll(z, cells - 1, 0))
        return z

    at_rim = jnp.where(core == 0, i == 0, i == tiles - 1)

    def near_step(n, carry):
        @pl.when(n == 4)
        def _():
            halo_up(0).wait_recv()

            @pl.when(core == 0)
            def _():
                halo_down(0).wait_recv()


        @pl.when(jnp.logical_not(jnp.logical_and(n == 4, at_rim)))
        def _():
            add_row(near, 0, n, outs)

        return carry

    lax.fori_loop(0, 6, near_step, 0)
    which = jnp.where(t == 0, 0, 1)

    def far_step(n, carry):
        @pl.when(jnp.logical_and(has_prev, n == 0))
        def _():
            onward(core).wait_recv()
            send_halo(1, core)

        @pl.when(jnp.logical_and(has_prev, n == 2))
        def _():
            @pl.when(core == 0)
            def _():
                back.wait_recv()

            @pl.when(core == 1)
            def _():
                across.wait_recv()
                back.start()
                onward(0).wait_recv()
                halo_up(1).start()

        add_row(far, which, n, 0)

        @pl.when(n == 1)
        def _():
            for dx in range(3):
                z = shifted(near[dx], dx)
                base[:, :outs] += z[:, outs:]
                base[:, outs:] += z[:, :outs] + z[:, outs:]

        return carry

    lax.fori_loop(0, 4, far_step, 0)
    for dx in range(3):
        z = shifted(far[dx], dx)
        base[:, :outs] += z[:, :outs] + z[:, outs:]
        base[:, outs:] += z[:, :outs]

    place = lax.broadcasted_iota(jnp.int32, (cols, 1), 0)

    def last_step(k, carry):
        n = jnp.where(core == 0, k, 9 - k)

        @pl.when(jnp.logical_and(has_prev, jnp.logical_and(core == 0, k == 4)))
        def _():
            halo_down(1).wait_recv()

        @pl.when(jnp.logical_and(has_prev, k == 5))
        def _():
            halo_up(1).wait_recv()

        source, target, dy = visit(n)
        row = act[which, source]
        row = jnp.where(jnp.logical_and(n == 4, at_rim), jnp.zeros_like(row), row)
        part = pl.ds(pl.multiple_of(target * cols, cols), cols)
        even = base[part, :outs]
        odd = base[part, outs:]
        for dx in range(3):
            z = jnp.dot(row, wc[dx, dy, :, :2 * outs], preferred_element_type=F32)
            if dx == 0:
                z = jnp.where(place == 0, 0.0, pltpu.roll(z, 1, 0))
            if dx == 2:
                z = jnp.where(place == cols - 1, 0.0, pltpu.roll(z, cols - 1, 0))
            even = even + (z[:, :outs] + z[:, outs:])
            odd = odd + z[:, :outs]
        out_ref[0, part, :] = even.astype(BF16)
        out_ref[1, part, :] = odd.astype(BF16)
        return carry

    lax.fori_loop(4, 6, last_step, 0)

    for h in range(2):
        for lane in range(2):
            first(h, lane).wait_send()
    own_to_sibling.wait_send()

    def drain(e, carry):
        for lane in range(2):
            @pl.when(e < steps - 2)
            def _():
                ring_copy(e, lane).wait_send()
        sib_copy(e).wait_send()
        return carry

    lax.fori_loop(1, steps, drain, 0)

    for d in range(1, half + 1):
        sums_right(d).wait_send()
    for d in range(1, half):
        sums_left(d).wait_send()
    sums_across.wait_send()
    halo_up(0).wait_send()
    halo_down(0).wait_send()

    @pl.when(has_prev)
    def _():
        halo_up(1).wait_send()

        @pl.when(core == 1)
        def _():
            halo_down(1).wait_send()
            back.wait_send()

    @pl.when(has_next)
    def _():
        onward(0).wait_send()

        @pl.when(core == 1)
        def _():
            onward(1).wait_send()
            across.wait_send()


def per_device(
    spans, tiles, features, norm_gain, query_weight, key_weight, value_weight, out_weight, conv_weight, skip_weight
):
    frames, rows, cols, channels = features.shape
    outs = conv_weight.shape[-1]
    cells = rows * cols
    steps = tiles // 2
    hbm = pl.BlockSpec(memory_space=pltpu.HBM)
    dma = pltpu.SemaphoreType.DMA
    operands = (
        features.reshape(rows, cols, channels), norm_gain.reshape(1, channels),
        query_weight, key_weight, value_weight, out_weight, conv_weight, skip_weight,
    )
    operands = [pltpu.with_memory_space_constraint(operand, pltpu.HBM) for operand in operands]
    out = pl.pallas_call(
        functools.partial(kernel, spans, tiles),
        out_shape=jax.ShapeDtypeStruct((2, cells, outs), BF16),
        in_specs=[hbm] * 8,
        out_specs=pl.BlockSpec(memory_space=pltpu.VMEM),
        scratch_shapes=[
            pltpu.VMEM((steps, 4, cols, channels), BF16),
            pltpu.VMEM((cells, channels), BF16),
            pltpu.VMEM((cells, channels), F32),
            pltpu.VMEM((cells, 128), F32),
            pltpu.VMEM((cells, 128), F32),
            pltpu.VMEM((steps + 2, 1, 128), F32),
            pltpu.VMEM((8, channels), F32),
            pltpu.VMEM((1, channels), F32),
            pltpu.VMEM((channels, channels), BF16),
            pltpu.VMEM((channels, channels), BF16),
            pltpu.VMEM((channels, channels), BF16),
            pltpu.VMEM((channels, channels), BF16),
            pltpu.VMEM((channels, channels), BF16),
            pltpu.VMEM((channels, outs), BF16),
            pltpu.VMEM((2, 4, cols, channels), BF16),
            pltpu.VMEM((cells, channels), BF16),
            pltpu.VMEM((3, cells, 2 * outs), F32),
            pltpu.VMEM((3, cells, 2 * outs), F32),
            pltpu.VMEM((cells, 2 * outs), F32),
            pltpu.VMEM((3, 3, channels, 3 * outs), BF16),
            dma((steps, 2)), dma((steps, 2)), dma((steps,)), dma((steps,)), dma((steps + 1,)), dma((steps + 1,)), dma((7,)),
            dma((8,)), dma((8,)), dma((27,)),
        ],
        compiler_params=pltpu.CompilerParams(
            collective_id=0, has_side_effects=True, vmem_limit_bytes=50 * 1024 * 1024
        ),
        name="mid_block_decode",
    )(*operands)
    return out.reshape(2 * frames, rows, cols, outs)


def solution(mesh):
    spans, tiles = mesh.shape["tm"], mesh.shape["tile"]
    in_specs = (P("tm", "tile", None, None), P(), P(), P(), P(), P(), P(), P())
    return jax.shard_map(
        functools.partial(per_device, spans, tiles), mesh=mesh, in_specs=in_specs,
        out_specs=P("tm", "tile", None, None), check_vma=False,
    )
```

```python
import functools
import math

import jax
import jax.numpy as jnp
from jax import lax
from jax.experimental import pallas as pl
from jax.experimental.pallas import tpu as pltpu
from jax.sharding import PartitionSpec as P

GROUPS = 32
EPS = 1e-06
MESH = pl.DeviceIdType.MESH
F32 = jnp.float32
BF16 = jnp.bfloat16


def group_sum(v, width):
    lanes = v.shape[-1]
    lane = lax.broadcasted_iota(jnp.int32, v.shape, 1)
    step = 1
    while step < width:
        above = pltpu.roll(v, lanes - step, 1)
        below = pltpu.roll(v, step, 1)
        v = v + jnp.where((lane & step) == 0, above, below)
        step *= 2
    return v


def remote(src, dst, send, recv, where):
    return pltpu.make_async_remote_copy(
        src_ref=src, dst_ref=dst, send_sem=send, recv_sem=recv, device_id=where, device_id_type=MESH
    )


def kernel(
    spans, tiles, x_hbm, gain_hbm, wq_hbm, wk_hbm, wv_hbm, wo_hbm, wc_hbm, ws_hbm, out_ref,
    slots, q2, acc, peak, total, stats, ab, gain, wq, wk, wv, wo, wvo, ws,
    act, mid, near, far, base, wc,
    ring_send, ring_recv, sib_send, sib_recv, st_send, st_recv, load_sem, edge_send, edge_recv, conv_sem,
):
    rows, cols, channels = x_hbm.shape
    outs = ws.shape[1]
    cells = rows * cols
    width = channels // GROUPS
    blocks = channels // 128
    steps = tiles // 2

    t = lax.axis_index("tm")
    i = lax.axis_index("tile")
    y = i // 2
    core = i - 2 * y
    right = lax.rem(i + 2, tiles)
    left = lax.rem(i + tiles - 2, tiles)
    sibling = 2 * y + 1 - core
    above = lax.rem(i + tiles - 1, tiles)
    below = lax.rem(i + 1, tiles)
    t_next = lax.rem(t + 1, spans)
    t_prev = lax.rem(t + spans - 1, spans)
    has_next = t < spans - 1
    has_prev = t > 0

    loads = [
        pltpu.make_async_copy(x_hbm, slots.at[0, pl.ds(0, 2)], load_sem.at[0]),
        pltpu.make_async_copy(wq_hbm, wq, load_sem.at[1]),
        pltpu.make_async_copy(wk_hbm, wk, load_sem.at[2]),
        pltpu.make_async_copy(gain_hbm, gain, load_sem.at[3]),
        pltpu.make_async_copy(wv_hbm, wv, load_sem.at[4]),
        pltpu.make_async_copy(wo_hbm, wo, load_sem.at[5]),
        pltpu.make_async_copy(ws_hbm, ws, load_sem.at[6]),
    ]
    loads[0].start()

    barrier = pltpu.get_barrier_semaphore()

    edge_peer = jnp.where(core == 0, above, below)
    for peer in (right, left, sibling, edge_peer):
        pl.semaphore_signal(barrier, inc=1, device_id=(t, peer), device_id_type=MESH)

    @pl.when(has_prev)
    def _():
        pl.semaphore_signal(barrier, inc=1, device_id=(t_prev, i), device_id_type=MESH)

    loads[0].wait()
    pl.semaphore_wait(barrier, 4 + jnp.where(has_next, 1, 0))

    def first(h, lane):
        row = h if lane == 0 else 1 - h
        return remote(
            slots.at[0, row], slots.at[1 + h, lane], ring_send.at[1 + h, lane], ring_recv.at[1 + h, lane],
            (t, right if lane == 0 else left),
        )

    for lane in range(2):
        first(0, lane).start()
    own_to_sibling = remote(
        slots.at[0, pl.ds(0, 2)], slots.at[0, pl.ds(2, 2)], sib_send.at[0], sib_recv.at[0], (t, sibling)
    )
    own_to_sibling.start()

    own = slots[0, 0:2].reshape(cells, channels).astype(F32)
    sums = jnp.sum(own, axis=0, keepdims=True)
    squares = jnp.sum(own * own, axis=0, keepdims=True)
    sums = group_sum(jnp.broadcast_to(sums, (8, channels)), width)
    squares = group_sum(jnp.broadcast_to(squares, (8, channels)), width)
    lane_of = lax.broadcasted_iota(jnp.int32, (8, 128), 1) & (width - 1)
    packed = jnp.zeros((8, 128), F32)
    for k in range(2 * blocks):
        source = sums if k < blocks else squares
        b = k % blocks
        packed = jnp.where(lane_of == k, source[:, b * 128:(b + 1) * 128], packed)
    stats[tiles // 2] = packed[0:1]

    half = steps // 2

    def sums_right(d):
        return remote(
            stats.at[d - 1], stats.at[d], st_send.at[d], st_recv.at[d], (t, right)
        )

    def sums_left(d):
        source = jnp.where(d == 1, 0, half + d - 1)
        return remote(
            stats.at[source], stats.at[half + d], st_send.at[half + d], st_recv.at[half + d], (t, left)
        )

    sums_across = remote(stats.at[steps], stats.at[steps + 1], st_send.at[steps], st_recv.at[steps], (t, sibling))

    def relay(d):
        sums_right(d).wait_recv()
        sums_right(d + 1).start()
        sums_left(d).wait_recv()

        @pl.when(d < half - 1)
        def _():
            sums_left(d + 1).start()

    sums_across.start()
    sums_across.wait_recv()
    stats[0] = stats[steps] + stats[steps + 1]
    sums_right(1).start()
    sums_left(1).start()
    for lane in range(2):
        first(1, lane).start()
    for copy in loads[1:]:
        copy.start()

    def ring_copy(e, lane):
        return remote(
            slots.at[e, lane], slots.at[e + 2, lane], ring_send.at[e + 2, lane], ring_recv.at[e + 2, lane],
            (t, right if lane == 0 else left),
        )

    def ring_arrival(e, lane):
        return remote(
            slots.at[e, lane], slots.at[e, lane], ring_send.at[e, lane], ring_recv.at[e, lane],
            (t, right if lane == 0 else left),
        )

    def sib_copy(e):
        return remote(
            slots.at[e, pl.ds(0, 2)], slots.at[e, pl.ds(2, 2)], sib_send.at[e], sib_recv.at[e], (t, sibling)
        )

    def prepare():
        sums_right(half).wait_recv()
        whole = stats[0]
        for k in range(1, steps):
            whole = whole + stats[k]
        whole = jnp.broadcast_to(whole, (8, 128))
        spread = [group_sum(jnp.where(lane_of == k, whole, 0.0), width) for k in range(2 * blocks)]
        population = float(tiles * cells * width)
        mean = jnp.concatenate(spread[:blocks], axis=1)[0:1] / population
        var = jnp.concatenate(spread[blocks:], axis=1)[0:1] / population - mean * mean
        rstd = lax.rsqrt(var + EPS)
        loads[3].wait()
        scaled = rstd * gain[...]
        ab[0:1] = scaled
        ab[1:2] = -mean * scaled
        block = slots[0, 0:2].reshape(cells, channels).astype(F32)
        normed = (((block - mean) * rstd) * gain[...]).astype(BF16)
        loads[1].wait()
        queries = jnp.dot(normed, wq[...], preferred_element_type=F32).astype(BF16)
        loads[2].wait()
        inner = lax.dot_general(queries, wk[...], (((1,), (1,)), ((), ())), preferred_element_type=F32)
        scale = channels ** (-0.5) * math.log2(math.e)
        q2[...] = (inner * (scaled * scale)).astype(BF16)
        acc[...] = jnp.zeros_like(acc)
        total[...] = jnp.zeros_like(total)
        peak[...] = jnp.full_like(peak, -jnp.inf)

    everything = pl.ds(0, cells)

    def attend(e, begin, count, part=everything):
        keys = slots[e, begin:begin + count].reshape(count * cols, channels)
        scores = lax.dot_general(q2[part, :], keys, (((1,), (1,)), ((), ())), preferred_element_type=F32)
        before = peak[part, 0:1]
        now = jnp.maximum(before, jnp.max(scores, axis=1, keepdims=True))
        fade = jnp.exp2(before - now)
        weights = jnp.exp2(scores - now).astype(BF16)
        peak[part, :] = jnp.broadcast_to(now, (now.shape[0], 128))
        total[part, :] = total[part, :] * fade + jnp.sum(weights.astype(F32), axis=1, keepdims=True)
        acc[part, :] = acc[part, :] * fade + jnp.dot(weights, keys, preferred_element_type=F32)

    def arrive(e):
        for lane in range(2):
            ring_arrival(e, lane).wait_recv()

            @pl.when(e < steps - 2)
            def _():
                ring_copy(e, lane).start()

        sib_copy(e).start()

    def attend_step(e, carry):
        sib_copy(e).wait_recv()
        attend(e, 0, 4)
        return carry

    def tap(k):
        dt = k // 9
        dy = (k - 9 * dt) // 3
        dx = k - 9 * dt - 3 * dy
        column = pl.multiple_of(dt * outs, outs)
        return pltpu.make_async_copy(wc_hbm.at[dt, dy, dx], wc.at[dx, dy, :, pl.ds(column, outs)], conv_sem.at[k])

    def load_tap(k, carry):
        tap(k).start()
        return carry

    def take_tap(k, carry):
        tap(k).wait()
        return carry

    def tap(k):
        dt = k // 9
        dy = (k - 9 * dt) // 3
        dx = k - 9 * dt - 3 * dy
        column = pl.multiple_of(dt * outs, outs)
        return pltpu.make_async_copy(wc_hbm.at[dt, dy, dx], wc.at[dx, dy, :, pl.ds(column, outs)], conv_sem.at[k])

    def load_tap(k, carry):
        tap(k).start()
        return carry

    def take_tap(k, carry):
        tap(k).wait()
        return carry

    def gather_step(e, carry):
        @pl.when(e < half)
        def _():
            relay(e)

        arrive(e)

        @pl.when(e == 2)
        def _():
            lax.fori_loop(0, 27, load_tap, 0)
            loads[4].wait()
            loads[5].wait()
            wvo[...] = jnp.dot(wv[...], wo[...], preferred_element_type=F32).astype(BF16)

        @pl.when(e == half)
        def _():
            prepare()

        low = jnp.where(e <= half, 0, jnp.where(e == half + 1, 1, half))
        high = jnp.where(e <= half, 1, jnp.where(e == half + 1, half, steps - 2))
        high = jnp.where(e < half, 0, high)
        high = jnp.where(e == steps - 1, low, high)
        lax.fori_loop(low, high, attend_step, 0)
        return carry

    lax.fori_loop(1, steps, gather_step, 0)
    attend_step(steps - 2, 0)
    attend(steps - 1, 0, 2)
    sib_copy(steps - 1).wait_recv()

    def halo_up(which):
        return remote(
            act.at[which, 1], act.at[which, 3], edge_send.at[2 * which], edge_recv.at[2 * which], (t, above)
        )

    def halo_down(which):
        return remote(
            act.at[which, 2], act.at[which, 0], edge_send.at[2 * which + 1], edge_recv.at[2 * which + 1], (t, below)
        )

    def onward(row):
        return remote(
            act.at[0, 1 + row], act.at[1, 1 + row], edge_send.at[4 + row], edge_recv.at[4 + row], (t_next, i)
        )

    across = remote(act.at[0, 0], act.at[1, 0], edge_send.at[6], edge_recv.at[6], (t_next, i))
    back = remote(act.at[1, 0], act.at[1, 2], edge_send.at[7], edge_recv.at[7], (t, above))

    def send_halo(which, row):
        @pl.when(row == 0)
        def _():
            halo_up(which).start()

        @pl.when(row == 1)
        def _():
            halo_down(which).start()

    def finish(k, carry):
        row = k + core - 2 * k * core
        part = pl.ds(pl.multiple_of(row * cols, cols), cols)
        attend(steps - 1, 2, 2, part)
        mixed = (acc[part, :] * (1.0 / total[part, 0:1]) * ab[0:1] + ab[1:2]).astype(BF16)
        change = jnp.dot(mixed, wvo[...], preferred_element_type=F32)
        mid_row = (slots[0, row].astype(F32) + change).astype(BF16)
        mid[part, :] = mid_row
        wide = mid_row.astype(F32)
        act[0, 1 + row] = (wide * (1.0 / (1.0 + jnp.exp(-wide)))).astype(BF16)

        @pl.when(jnp.logical_and(has_next, k == 0))
        def _():
            onward(row).start()

        send_halo(0, row)
        return carry

    lax.fori_loop(0, 2, finish, 0)

    @pl.when(core == 1)
    def _():
        halo_down(0).wait_recv()

        @pl.when(has_next)
        def _():
            across.start()
            onward(0).start()


    loads[6].wait()
    skip = jnp.dot(mid[...], ws[...], preferred_element_type=F32)
    base[:, :outs] = skip
    base[:, outs:] = skip
    near[...] = jnp.zeros_like(near)
    far[...] = jnp.zeros_like(far)
    lax.fori_loop(0, 27, take_tap, 0)

    def visit(n):
        own = n < 4
        first = lax.rem(n, 2) == 0
        inner = n // 2
        mine = jnp.where(inner == 0, 1 + core, 2 - core)
        halo = jnp.where(first, 3 * core, 3 - 3 * core)
        source = jnp.where(own, mine, halo)
        same = jnp.where(inner == 0, core, 1 - core)
        target = jnp.where(own, jnp.where(first, same, 1 - same), jnp.where(first, core, 1 - core))
        return source, target, source - target

    def add_row(sums, which, n, start):
        source, target, dy = visit(n)
        row = act[which, source]
        part = pl.ds(pl.multiple_of(target * cols, cols), cols)
        for dx in range(3):
            sums[dx, part, :] += jnp.dot(row, wc[dx, dy, :, start:start + 2 * outs], preferred_element_type=F32)

    position = lax.rem(lax.broadcasted_iota(jnp.int32, (cells, 1), 0), cols)

    def shifted(z, dx):
        if dx == 0:
            return jnp.where(position == 0, 0.0, pltpu.roll(z, 1, 0))
        if dx == 2:
            return jnp.where(position == cols - 1, 0.0, pltpu.roll(z, cells - 1, 0))
        return z

    at_rim = jnp.where(core == 0, i == 0, i == tiles - 1)

    def near_step(n, carry):
        @pl.when(n == 4)
        def _():
            halo_up(0).wait_recv()

            @pl.when(core == 0)
            def _():
                halo_down(0).wait_recv()


        @pl.when(jnp.logical_not(jnp.logical_and(n == 4, at_rim)))
        def _():
            add_row(near, 0, n, outs)

        return carry

    lax.fori_loop(0, 6, near_step, 0)
    which = jnp.where(t == 0, 0, 1)

    def far_step(n, carry):
        @pl.when(jnp.logical_and(has_prev, n == 0))
        def _():
            onward(core).wait_recv()
            send_halo(1, core)

        @pl.when(jnp.logical_and(n == 2, core == 0))
        def _():
            @pl.when(has_prev)
            def _():
                back.wait_recv()

        @pl.when(jnp.logical_and(n == 2, core == 1))
        def _():
            @pl.when(has_prev)
            def _():
                across.wait_recv()
                back.start()

            add_row(far, which, 5, 0)

            @pl.when(has_prev)
            def _():
                onward(0).wait_recv()
                halo_up(1).start()

        add_row(far, which, n, 0)

        @pl.when(n == 1)
        def _():
            for dx in range(3):
                z = shifted(near[dx], dx)
                base[:, :outs] += z[:, outs:]
                base[:, outs:] += z[:, :outs] + z[:, outs:]

        return carry

    lax.fori_loop(0, 4, far_step, 0)
    for dx in range(3):
        z = shifted(far[dx], dx)
        base[:, :outs] += z[:, :outs] + z[:, outs:]
        base[:, outs:] += z[:, :outs]

    place = lax.broadcasted_iota(jnp.int32, (cols, 1), 0)

    @pl.when(core == 1)
    def _():
        out_ref[0, 0:cols, :] = base[0:cols, :outs].astype(BF16)
        out_ref[1, 0:cols, :] = base[0:cols, outs:].astype(BF16)

    def last_step(k, carry):
        n = jnp.where(core == 0, k, 4)

        @pl.when(jnp.logical_and(has_prev, jnp.logical_and(core == 0, k == 4)))
        def _():
            halo_down(1).wait_recv()

        @pl.when(jnp.logical_and(has_prev, k == 5))
        def _():
            halo_up(1).wait_recv()

        source, target, dy = visit(n)
        row = act[which, source]
        row = jnp.where(jnp.logical_and(n == 4, at_rim), jnp.zeros_like(row), row)
        part = pl.ds(pl.multiple_of(target * cols, cols), cols)
        even = base[part, :outs]
        odd = base[part, outs:]
        for dx in range(3):
            z = jnp.dot(row, wc[dx, dy, :, :2 * outs], preferred_element_type=F32)
            if dx == 0:
                z = jnp.where(place == 0, 0.0, pltpu.roll(z, 1, 0))
            if dx == 2:
                z = jnp.where(place == cols - 1, 0.0, pltpu.roll(z, cols - 1, 0))
            even = even + (z[:, :outs] + z[:, outs:])
            odd = odd + z[:, :outs]
        out_ref[0, part, :] = even.astype(BF16)
        out_ref[1, part, :] = odd.astype(BF16)
        return carry

    lax.fori_loop(4 + core, 6, last_step, 0)

    for h in range(2):
        for lane in range(2):
            first(h, lane).wait_send()
    own_to_sibling.wait_send()

    def drain(e, carry):
        for lane in range(2):
            @pl.when(e < steps - 2)
            def _():
                ring_copy(e, lane).wait_send()
        sib_copy(e).wait_send()
        return carry

    lax.fori_loop(1, steps, drain, 0)

    for d in range(1, half + 1):
        sums_right(d).wait_send()
    for d in range(1, half):
        sums_left(d).wait_send()
    sums_across.wait_send()
    halo_up(0).wait_send()
    halo_down(0).wait_send()

    @pl.when(has_prev)
    def _():
        halo_up(1).wait_send()

        @pl.when(core == 1)
        def _():
            halo_down(1).wait_send()
            back.wait_send()

    @pl.when(has_next)
    def _():
        onward(0).wait_send()

        @pl.when(core == 1)
        def _():
            onward(1).wait_send()
            across.wait_send()


def per_device(
    spans, tiles, features, norm_gain, query_weight, key_weight, value_weight, out_weight, conv_weight, skip_weight
):
    frames, rows, cols, channels = features.shape
    outs = conv_weight.shape[-1]
    cells = rows * cols
    steps = tiles // 2
    hbm = pl.BlockSpec(memory_space=pltpu.HBM)
    dma = pltpu.SemaphoreType.DMA
    operands = (
        features.reshape(rows, cols, channels), norm_gain.reshape(1, channels),
        query_weight, key_weight, value_weight, out_weight, conv_weight, skip_weight,
    )
    operands = [pltpu.with_memory_space_constraint(operand, pltpu.HBM) for operand in operands]
    out = pl.pallas_call(
        functools.partial(kernel, spans, tiles),
        out_shape=jax.ShapeDtypeStruct((2, cells, outs), BF16),
        in_specs=[hbm] * 8,
        out_specs=pl.BlockSpec(memory_space=pltpu.VMEM),
        scratch_shapes=[
            pltpu.VMEM((steps, 4, cols, channels), BF16),
            pltpu.VMEM((cells, channels), BF16),
            pltpu.VMEM((cells, channels), F32),
            pltpu.VMEM((cells, 128), F32),
            pltpu.VMEM((cells, 128), F32),
            pltpu.VMEM((steps + 2, 1, 128), F32),
            pltpu.VMEM((8, channels), F32),
            pltpu.VMEM((1, channels), F32),
            pltpu.VMEM((channels, channels), BF16),
            pltpu.VMEM((channels, channels), BF16),
            pltpu.VMEM((channels, channels), BF16),
            pltpu.VMEM((channels, channels), BF16),
            pltpu.VMEM((channels, channels), BF16),
            pltpu.VMEM((channels, outs), BF16),
            pltpu.VMEM((2, 4, cols, channels), BF16),
            pltpu.VMEM((cells, channels), BF16),
            pltpu.VMEM((3, cells, 2 * outs), F32),
            pltpu.VMEM((3, cells, 2 * outs), F32),
            pltpu.VMEM((cells, 2 * outs), F32),
            pltpu.VMEM((3, 3, channels, 3 * outs), BF16),
            dma((steps, 2)), dma((steps, 2)), dma((steps,)), dma((steps,)), dma((steps + 1,)), dma((steps + 1,)), dma((7,)),
            dma((8,)), dma((8,)), dma((27,)),
        ],
        compiler_params=pltpu.CompilerParams(
            collective_id=0, has_side_effects=True, vmem_limit_bytes=50 * 1024 * 1024
        ),
        name="mid_block_decode",
    )(*operands)
    return out.reshape(2 * frames, rows, cols, outs)


def solution(mesh):
    spans, tiles = mesh.shape["tm"], mesh.shape["tile"]
    in_specs = (P("tm", "tile", None, None), P(), P(), P(), P(), P(), P(), P())
    return jax.shard_map(
        functools.partial(per_device, spans, tiles), mesh=mesh, in_specs=in_specs,
        out_specs=P("tm", "tile", None, None), check_vma=False,
    )
```
